512 devices in a mesh: dp: 8 (over z_lo, x), region: 64 (over y, z_hi, core).
Axes of the slice: x: 4, y: 8, z: 8 (z_hi: 4, z_lo: 2; z = z_hi * 2 + z_lo), core: 2. Of those that a mesh axis runs over, the one named last changes fastest.
Arguments:
- queries: bfloat16 [8, 8192, 1280], P('dp', 'region'), may hold values from -5 to 5
- keys: bfloat16 [8, 8192, 1280], P('dp', 'region'), may hold values from -5 to 5
- values: bfloat16 [8, 8192, 1280], P('dp', 'region'), may hold values from -6 to 6
- attn_out: bfloat16 [8, 8192, 1280], P('dp', 'region'), may hold values from -0.125 to 0.125
- d_out: bfloat16 [8, 8192, 2560], P('dp', 'region'), may hold values from -6 to 6
- w_out: bfloat16 [1280, 2560], P('dp'), may hold values from -0.15625 to 0.15625
- adjacency: int32 [64, 4, 12], P('region'), may hold values from 0 to 1, as said below
- counts: int32 [64], P('region'), may hold values from 1 to 4, as said below
Outputs:
- d_queries: bfloat16 [8, 8192, 1280], P('dp', 'region')
- d_keys: bfloat16 [8, 8192, 1280], P('dp', 'region')
- d_values: bfloat16 [8, 8192, 1280], P('dp', 'region')
- d_weight: bfloat16 [1280, 2560], P('dp')
The draws below stay inside these ranges and needn't reach their ends.
Inputs may be any that keep to these rules, and one draw needn't show every extreme that they name: Region r has 4 token blocks, of which the first counts[r] are live; in some region all 4 are live. adjacency[r, a, j] = 1 lets query block a of region r see key block j % 4 of region (r + j // 4 - 1) mod 64; entry j = 4 + a is 1.
All inputs are finite; a program needn't handle non-finite values.
Results may differ from the reference program's by a relative error of at most 0.007.
Values may be sent and summed in bfloat16 or wider, within the bound.
No kernel may reach another device: no remote copies, remote signals or barrier semaphores. Data moves between devices by JAX's collectives and lax.ppermute only.
A program may use at most 64 MiB of HBM per device.

```python
import math
import jax
import jax.numpy as jnp
from jax import lax

D = 2560
HEADS = 8
HD = 160
BLK = 4
BROWS = 32
REGIONS = 64
TOKENS = 8192
SAMPLES = 8
HW = 1280


def drawn_pair(key):
    shape = (SAMPLES, TOKENS, HEADS * HD)
    key_query, key_key = jax.random.split(jax.random.fold_in(key, 11), 2)
    query_draw = jnp.clip(jax.random.normal(key_query, shape, jnp.float32), -4.0, 4.0)
    key_draw = jnp.clip(jax.random.normal(key_key, shape, jnp.float32), -4.0, 4.0)
    return (query_draw, key_draw)


def draw_queries(key, part):
    return drawn_pair(key)[0].astype(jnp.bfloat16)


def draw_keys(key, part):
    return drawn_pair(key)[1].astype(jnp.bfloat16)


def draw_adjacency(key, part):
    bits = jax.random.randint(jax.random.fold_in(key, 3), (REGIONS, BLK, 3 * BLK), 0, 2)
    own_block = jnp.arange(3 * BLK)[None, :] == BLK + jnp.arange(BLK)[:, None]
    return jnp.where(own_block[None], 1, bits).astype(jnp.int32)


def draw_counts(key, part):
    region_index = jnp.arange(REGIONS)
    half_cycle = REGIONS // 2
    position = region_index % half_cycle
    distance = jnp.minimum(position, half_cycle - position)
    base = 1 + (BLK - 1) * distance * 4 // REGIONS
    jitter = jax.random.randint(jax.random.fold_in(key, 5), (REGIONS,), 0, 2)
    ragged = jnp.clip(base + jitter, 1, BLK)
    return jnp.where(distance == REGIONS // 4, BLK, ragged).astype(jnp.int32)


def level_of(stream_key, shape, pieces, least, high):
    loudness = 1.0
    for dim, blocks in pieces:
        steps = jax.random.uniform(jax.random.fold_in(jax.random.fold_in(stream_key, 6), dim), (blocks,), jnp.float32, least / len(pieces), high / len(pieces))
        loudness = loudness * jnp.repeat(jnp.exp(steps), shape[dim] // blocks).reshape((-1,) + (1,) * (len(shape) - 1 - dim))
    return loudness


def noise(stream_key, dims, scale, bound, cuts=(), held_as=jnp.bfloat16):
    values = jax.random.normal(stream_key, dims, jnp.float32) * scale
    if len(cuts) > 0:
        values = level_of(stream_key, dims, cuts, -0.22, 0.18) * values
    return jnp.clip(values, min=-bound, max=bound).astype(held_as)


def setup_inputs(seed: int = 0) -> dict:
    key_list = jax.random.split(jax.random.key(seed), 9)
    return {
        "queries": draw_queries(jax.random.fold_in(key_list[8], 71), 0),
        "keys": draw_keys(jax.random.fold_in(key_list[8], 71), 0),
        "values": noise(key_list[2], (SAMPLES, TOKENS, HW), 1.0, 6.0, ((0, 8), (1, 64))),
        "attn_out": noise(key_list[3], (SAMPLES, TOKENS, HW), (2.0 / (SAMPLES * TOKENS) ** 0.5), 0.125, ((0, 8), (1, 64))),
        "d_out": noise(key_list[4], (SAMPLES, TOKENS, D), 1.0, 6.0, ((0, 8), (1, 64))),
        "w_out": noise(key_list[5], (HW, D), HW ** -0.5, 0.15625, ((0, 8),)),
        "adjacency": draw_adjacency(jax.random.fold_in(key_list[8], 71), 0),
        "counts": draw_counts(jax.random.fold_in(key_list[8], 71), 0),
    }


def window(blocks):
    return jnp.concatenate([jnp.roll(blocks, 1, axis=0), blocks, jnp.roll(blocks, -1, axis=0)], axis=1)

def reference(queries, keys, values, attn_out, d_out, w_out, adjacency, counts):
    tok_rows = BLK * BROWS
    width = HEADS * HD
    scale = 1.0 / math.sqrt(HD)
    high = lax.Precision.HIGHEST
    live_blocks = jnp.arange(BLK)[None, :] < counts[:, None]
    live_rows = jnp.repeat(live_blocks, BROWS, axis=1).reshape(REGIONS * tok_rows)
    grads = d_out * live_rows[None, :, None].astype(jnp.bfloat16)
    d_attn = jnp.dot(grads.reshape(-1, D), w_out.T, preferred_element_type=jnp.float32)
    d_attn = d_attn.astype(jnp.bfloat16).reshape(queries.shape)
    d_weight = jnp.dot(attn_out.reshape(-1, width).T, grads.reshape(-1, D), preferred_element_type=jnp.float32)
    d_weight = d_weight.astype(jnp.bfloat16)
    own_block = jnp.arange(3 * BLK)[None, :] == BLK + jnp.arange(BLK)[:, None]
    live_window = window(live_blocks)
    allowed_blocks = (adjacency == 1) & live_window[:, None, :] | own_block[None]
    allowed = jnp.repeat(jnp.repeat(allowed_blocks, BROWS, axis=1), BROWS, axis=2)

    def fold(win_terms):
        middle = win_terms[:, tok_rows:2 * tok_rows]
        return middle + jnp.roll(win_terms[:, :tok_rows], -1, axis=0) + jnp.roll(win_terms[:, 2 * tok_rows:], 1, axis=0)

    def one_sample(items):
        parts = [item.reshape(REGIONS, tok_rows, HEADS, HD).astype(jnp.float32) for item in items]
        query_rows, key_rows, value_rows, out_rows, grad_rows = parts
        key_window = window(key_rows)
        value_window = window(value_rows)
        scores = jnp.einsum('rqhc,rkhc->rhqk', query_rows, key_window, precision=high) * scale
        masked = jnp.where(allowed[:, None], scores, -1e+30)
        maxima = lax.optimization_barrier(jnp.max(masked, axis=-1))
        lse = maxima + jnp.log(lax.optimization_barrier(jnp.sum(jnp.exp(masked - maxima[..., None]), axis=-1)))
        probs = jnp.exp(masked - lse[..., None])
        probs_b = lax.optimization_barrier(probs.astype(jnp.bfloat16)).astype(jnp.float32)
        delta = jnp.einsum('rqhc,rqhc->rhq', grad_rows, out_rows, precision=high)
        dvalue_win = jnp.einsum('rhqk,rqhc->rkhc', probs_b, grad_rows, precision=high)
        dprobs = jnp.einsum('rqhc,rkhc->rhqk', grad_rows, value_window, precision=high)
        dscores = probs * (dprobs - delta[..., None]) * scale
        dscores = lax.optimization_barrier(dscores.astype(jnp.bfloat16)).astype(jnp.float32)
        dquery = jnp.einsum('rhqk,rkhc->rqhc', dscores, key_window, precision=high)
        dkey_win = jnp.einsum('rhqk,rqhc->rkhc', dscores, query_rows, precision=high)
        flat = (REGIONS * tok_rows, width)
        return (dquery.reshape(flat).astype(jnp.bfloat16), fold(dkey_win).reshape(flat).astype(jnp.bfloat16), fold(dvalue_win).reshape(flat).astype(jnp.bfloat16))
    d_queries, d_keys, d_values = lax.map(one_sample, (queries, keys, values, attn_out, d_attn))
    return (d_queries, d_keys, d_values, d_weight)
```

```python
import functools
import math

import jax
import jax.numpy as jnp
from jax import lax
from jax.experimental import pallas as pl
from jax.experimental.pallas import tpu as pltpu
from jax.sharding import Mesh
from jax.sharding import PartitionSpec as P

HEADS = 8
HD = 160
BLK = 4
DP = ("z_lo", "x")
YZ = ("y", "z_hi")
REGION = ("y", "z_hi", "core")
BF = jnp.bfloat16
F32 = jnp.float32
LANES = 128
EXTRA = HD - LANES
SCALE = 1.0 / math.sqrt(HD)


def nn(a, b):
    return lax.dot_general(a, b, (((1,), (0,)), ((), ())), preferred_element_type=F32)


def nt(a, b):
    return lax.dot_general(a, b, (((1,), (1,)), ((), ())), preferred_element_type=F32)


def tn(a, b):
    return lax.dot_general(a, b, (((0,), (0,)), ((), ())), preferred_element_type=F32)


def pack(rows):
    low = rows[:, :LANES]
    high = rows[:, LANES:]
    below = jnp.concatenate([high[g * EXTRA : (g + 1) * EXTRA] for g in range(LANES // EXTRA)], 1)
    return jnp.concatenate([low, below], 0)


def unpack(tile):
    below = tile[LANES:]
    high = jnp.concatenate(
        [below[:, g * EXTRA : (g + 1) * EXTRA] for g in range(LANES // EXTRA)], 0
    )
    return jnp.concatenate([tile[:LANES], high], 1)


def head(ref, h):
    return ref[:, h * HD : (h + 1) * HD]


def prepare_body(counts, d_out, attn_out, keys, values, spread, out_cols, halo):
    rows, _ = d_out.shape
    live = lax.broadcasted_iota(jnp.int32, (rows, 1), 0) // (rows // BLK) < counts[0]
    grads = jnp.where(live, d_out[...], jnp.zeros((), BF))
    for s in range(spread.shape[0]):
        spread[s] = grads
    for h in range(HEADS):
        out_cols[h] = pack(head(attn_out, h))
    halo[0:rows] = keys[...]
    halo[rows : 2 * rows] = values[...]
    count = counts[0].astype(F32)
    halo[2 * rows :] = jnp.full((8, halo.shape[1]), count, F32).astype(BF)


def probs_body(counts, adjacency, queries, keys, behind, ahead, probs):
    rows = queries.shape[0]
    block = rows // BLK
    width = 3 * rows
    lane = lax.broadcasted_iota(jnp.int32, (1, width), 1)
    key_block = lane // block
    count = jnp.concatenate(
        [
            behind[2 * rows : 2 * rows + 1, :rows].astype(F32),
            jnp.full((1, rows), counts[0].astype(F32), F32),
            ahead[2 * rows : 2 * rows + 1, :rows].astype(F32),
        ],
        1,
    )
    live = (key_block % BLK).astype(F32) < count
    bias = []
    for a in range(BLK):
        seen = jnp.zeros((1, width), jnp.int32)
        for j in range(3 * BLK):
            seen = jnp.where(key_block == j, adjacency[a, j], seen)
        ok = jnp.logical_or(
            jnp.logical_and(seen == 1, live), key_block == BLK + a
        )
        bias.append(jnp.broadcast_to(jnp.where(ok, 1.0, 0.0), (block, width)))
    allowed = jnp.concatenate(bias, 0) > 0.5
    for h in range(HEADS):
        cols = slice(h * HD, (h + 1) * HD)
        window = jnp.concatenate([behind[0:rows, cols], keys[:, cols], ahead[0:rows, cols]], 0)
        scores = jnp.where(allowed, nt(queries[:, cols], window) * SCALE, -1e30)
        maxima = jnp.max(scores, axis=1, keepdims=True)
        terms = jnp.where(allowed, jnp.exp(scores - maxima), 0.0)
        probs[h] = terms / jnp.sum(terms, axis=1, keepdims=True)


def weight_body(out_cols, gathered, weight, acc):
    step = pl.program_id(0)
    samples, rows, width = gathered.shape
    cols = jnp.concatenate([unpack(out_cols[s]) for s in range(samples)], 0)
    part = tn(cols, gathered[...].reshape(samples * rows, width))

    @pl.when(step == 0)
    def _():
        acc[...] = part

    @pl.when(step > 0)
    def _():
        acc[...] += part

    @pl.when(step == pl.num_programs(0) - 1)
    def _():
        half = HD // 2
        for c in range(2):
            for j in range(width // LANES):
                weight[c, j] = acc[
                    c * half : (c + 1) * half, j * LANES : (j + 1) * LANES
                ].astype(BF)


def project_body(gathered, w_out, packed):
    samples, rows, width = gathered.shape
    part = nt(gathered[...].reshape(samples * rows, width), w_out[...])
    for s in range(samples):
        packed[s] = pack(part[s * rows : (s + 1) * rows]).astype(BF)


def attention_body(
    probs, packed, attn_out, queries, keys, values, behind, ahead,
    d_queries, own, to_behind, to_ahead,
):
    rows = queries.shape[0]
    for h in range(HEADS):
        cols = slice(h * HD, (h + 1) * HD)
        grad = unpack(packed[h])
        delta = jnp.sum(
            grad.astype(F32) * attn_out[:, cols].astype(F32), axis=1, keepdims=True
        )
        value_win = jnp.concatenate(
            [behind[rows : 2 * rows, cols], values[:, cols], ahead[rows : 2 * rows, cols]], 0
        )
        key_win = jnp.concatenate([behind[0:rows, cols], keys[:, cols], ahead[0:rows, cols]], 0)
        prob = probs[h]
        dprobs = nt(grad, value_win)
        dscores = (prob * (dprobs - delta) * SCALE).astype(BF)
        d_queries[:, cols] = nn(dscores, key_win).astype(BF)
        for which, (left, right) in enumerate(
            ((dscores, queries[:, cols]), (prob.astype(BF), grad))
        ):
            win = tn(left, right)
            to_behind[which, :, cols] = win[:rows].astype(BF)
            own[which, :, cols] = win[rows : 2 * rows]
            to_ahead[which, :, cols] = win[2 * rows :].astype(BF)


def finish_body(own, from_behind, from_ahead, d_keys, d_values):
    for which, out in enumerate((d_keys, d_values)):
        out[...] = (
            own[which] + from_behind[which].astype(F32) + from_ahead[which].astype(F32)
        ).astype(BF)


def vmem():
    return pl.BlockSpec(memory_space=pltpu.VMEM)


def smem():
    return pl.BlockSpec(memory_space=pltpu.SMEM)


def call(body, outs, specs, **options):
    return pl.pallas_call(
        body,
        out_shape=tuple(jax.ShapeDtypeStruct(shape, dtype) for shape, dtype in outs),
        in_specs=specs,
        out_specs=tuple(vmem() for _ in outs),
        compiler_params=pltpu.CompilerParams(vmem_limit_bytes=48 << 20),
        **options,
    )


def shift(value, by):
    length = lax.axis_size(REGION)
    return lax.ppermute(value, REGION, [(i, (i + by) % length) for i in range(length)])


def local(queries, keys, values, attn_out, d_out, w_out, adjacency, counts):
    queries, keys, values, attn_out, d_out = (
        a[0] for a in (queries, keys, values, attn_out, d_out)
    )
    rows, hw = queries.shape
    width = d_out.shape[1]
    samples = lax.axis_size(DP)
    tile = (samples, HD, LANES)
    spread, out_cols, halo = call(
        prepare_body,
        [((samples, rows, width), BF), (tile, BF), ((2 * rows + 8, hw), BF)],
        [smem(), vmem(), vmem(), vmem(), vmem()],
    )(counts, d_out, attn_out, keys, values)
    gathered = lax.all_to_all(spread, DP, 0, 0)
    out_cols = lax.all_to_all(out_cols, DP, 0, 0)
    behind = shift(halo, 1)
    ahead = shift(halo, -1)
    (probs,) = call(
        probs_body,
        [((HEADS, rows, 3 * rows), F32)],
        [smem(), smem(), vmem(), vmem(), vmem(), vmem()],
    )(counts, adjacency[0], queries, keys, behind, ahead)

    group = 2
    steps = samples // group
    halves = (2, width // LANES, HD // 2, LANES)
    weight = pl.pallas_call(
        weight_body,
        out_shape=jax.ShapeDtypeStruct(halves, BF),
        grid=(steps,),
        in_specs=[
            pl.BlockSpec((group, HD, LANES), lambda i: (i, 0, 0)),
            pl.BlockSpec((group, rows, width), lambda i: (i, 0, 0)),
        ],
        out_specs=pl.BlockSpec(halves, lambda i: (0, 0, 0, 0)),
        scratch_shapes=[pltpu.VMEM((HD, width), F32)],
        compiler_params=pltpu.CompilerParams(vmem_limit_bytes=48 << 20),
    )(out_cols, gathered)
    packed = pl.pallas_call(
        project_body,
        out_shape=jax.ShapeDtypeStruct(tile, BF),
        grid=(steps,),
        in_specs=[
            pl.BlockSpec((group, rows, width), lambda i: (i, 0, 0)),
            pl.BlockSpec((HD, width), lambda i: (0, 0)),
        ],
        out_specs=pl.BlockSpec((group, HD, LANES), lambda i: (i, 0, 0)),
        compiler_params=pltpu.CompilerParams(vmem_limit_bytes=48 << 20),
    )(gathered, w_out)
    packed = lax.all_to_all(packed, DP, 0, 0)

    members = lax.axis_size(YZ)
    flat = halves[1] * halves[2]
    share = -(-flat // (8 * members)) * 8
    pair = lax.all_to_all(weight, "core", 0, 0)
    half = jnp.sum(pair.astype(F32), axis=0).astype(BF).reshape(flat, LANES)
    half = jnp.pad(half, ((0, share * members - flat), (0, 0)))
    terms = lax.all_to_all(half.reshape(members, share, LANES), YZ, 0, 0)
    total = jnp.sum(terms.astype(F32), axis=0).astype(BF)
    total = lax.all_to_all(jnp.broadcast_to(total[None], (members, share, LANES)), YZ, 0, 0)
    total = total.reshape(members * share, LANES)[:flat]
    both = lax.all_to_all(jnp.broadcast_to(total[None], (2, flat, LANES)), "core", 0, 0)
    d_weight = both.reshape(halves).transpose(0, 2, 1, 3).reshape(HD, width)

    pairs = (2, rows, hw)
    d_queries, own, to_behind, to_ahead = call(
        attention_body,
        [((rows, hw), BF), (pairs, F32), (pairs, BF), (pairs, BF)],
        [vmem()] * 8,
    )(probs, packed, attn_out, queries, keys, values, behind, ahead)
    d_keys, d_values = call(
        finish_body, [((rows, hw), BF), ((rows, hw), BF)], [vmem()] * 3
    )(own, shift(to_ahead, 1), shift(to_behind, -1))
    return d_queries[None], d_keys[None], d_values[None], d_weight


def solution(mesh):
    parts = Mesh(mesh.devices.reshape(2, 4, 8, 4, 2), DP + REGION)
    rows = P(DP, REGION, None)
    return jax.shard_map(
        local,
        mesh=parts,
        in_specs=(rows, rows, rows, rows, rows, P(DP, None), P(REGION, None, None), P(REGION)),
        out_specs=(rows, rows, rows, P(DP, None)),
        check_vma=False,
    )
```

```python
import math

import jax
import jax.numpy as jnp
from jax import lax
from jax.experimental import pallas as pl
from jax.experimental.pallas import tpu as pltpu
from jax.sharding import Mesh
from jax.sharding import PartitionSpec as P

HEADS = 8
HD = 160
BLK = 4
DP = ("z_lo", "x")
REGION = ("y", "z_hi", "core")
BF = jnp.bfloat16
F32 = jnp.float32
LANES = 128
EXTRA = HD - LANES
SCALE = 1.0 / math.sqrt(HD)


def nn(a, b):
    return lax.dot_general(a, b, (((1,), (0,)), ((), ())), preferred_element_type=F32)


def nt(a, b):
    return lax.dot_general(a, b, (((1,), (1,)), ((), ())), preferred_element_type=F32)


def tn(a, b):
    return lax.dot_general(a, b, (((0,), (0,)), ((), ())), preferred_element_type=F32)


def pack(rows):
    low = rows[:, :LANES]
    high = rows[:, LANES:]
    below = jnp.concatenate([high[g * EXTRA : (g + 1) * EXTRA] for g in range(LANES // EXTRA)], 1)
    return jnp.concatenate([low, below], 0)


def unpack(tile):
    below = tile[LANES:]
    high = jnp.concatenate(
        [below[:, g * EXTRA : (g + 1) * EXTRA] for g in range(LANES // EXTRA)], 0
    )
    return jnp.concatenate([tile[:LANES], high], 1)


def head(ref, h):
    return ref[:, h * HD : (h + 1) * HD]


def prepare_body(
    counts, d_out, attn_out, keys, values, spread, halo,
    grads_in, attn_in, sending, tail, sem_in, sem_out, sem_halo,
):
    rows, width = d_out.shape
    loads = [
        pltpu.make_async_copy(d_out, grads_in, sem_in.at[0]),
        pltpu.make_async_copy(attn_out, attn_in, sem_in.at[1]),
    ]
    for copy in loads:
        copy.start()
    tail[...] = jnp.full(tail.shape, counts[0].astype(F32), F32).astype(BF)
    moves = [
        pltpu.make_async_copy(keys, halo.at[pl.ds(0, rows)], sem_halo.at[0]),
        pltpu.make_async_copy(values, halo.at[pl.ds(rows, rows)], sem_halo.at[1]),
        pltpu.make_async_copy(tail, halo.at[pl.ds(2 * rows, 8)], sem_halo.at[2]),
    ]
    loads[0].wait()
    live = lax.broadcasted_iota(jnp.int32, (rows, 1), 0) // (rows // BLK) < counts[0]
    grads = jnp.where(live, grads_in[...], jnp.zeros((), BF))
    for s in range(HEADS):
        sending[s, 0:rows] = grads
    loads[1].wait()
    stores = []
    for h in range(HEADS):
        tile = pack(head(attn_in, h))
        for j in range(width // LANES):
            sending[h, rows : rows + 8, j * LANES : (j + 1) * LANES] = tile[8 * j : 8 * j + 8]
        stores.append(pltpu.make_async_copy(sending.at[h], spread.at[h], sem_out.at[h]))
        stores[h].start()
    for copy in moves:
        copy.start()
    for copy in stores + moves:
        copy.wait()


def probs_body(counts, adjacency, queries, keys, behind, ahead, probs):
    rows = queries.shape[0]
    block = rows // BLK
    width = 3 * rows
    lane = lax.broadcasted_iota(jnp.int32, (1, width), 1)
    key_block = lane // block
    count = jnp.concatenate(
        [
            behind[2 * rows : 2 * rows + 1, :rows].astype(F32),
            jnp.full((1, rows), counts[0].astype(F32), F32),
            ahead[2 * rows : 2 * rows + 1, :rows].astype(F32),
        ],
        1,
    )
    live = (key_block % BLK).astype(F32) < count
    bias = []
    for a in range(BLK):
        seen = jnp.zeros((1, width), jnp.int32)
        for j in range(3 * BLK):
            seen = jnp.where(key_block == j, adjacency[a, j], seen)
        ok = jnp.logical_or(
            jnp.logical_and(seen == 1, live), key_block == BLK + a
        )
        bias.append(jnp.broadcast_to(jnp.where(ok, 1.0, 0.0), (block, width)))
    allowed = jnp.concatenate(bias, 0) > 0.5
    for h in range(HEADS):
        cols = slice(h * HD, (h + 1) * HD)
        window = jnp.concatenate([behind[0:rows, cols], keys[:, cols], ahead[0:rows, cols]], 0)
        scores = jnp.where(allowed, nt(queries[:, cols], window) * SCALE, -1e30)
        maxima = jnp.max(scores, axis=1, keepdims=True)
        terms = jnp.where(allowed, jnp.exp(scores - maxima), 0.0)
        probs[h] = terms / jnp.sum(terms, axis=1, keepdims=True)


def weight_body(gathered, weight, acc):
    step = pl.program_id(0)
    samples, _, width = gathered.shape
    tiles = width // LANES
    part = jnp.zeros(acc.shape, F32)
    cols = []
    for s in range(samples):
        below = [gathered[s, LANES:, j * LANES : (j + 1) * LANES] for j in range(tiles)]
        cols.append(unpack(jnp.concatenate(below, 0)))
    grads = gathered[:, :LANES, :].reshape(samples * LANES, width)
    part = tn(jnp.concatenate(cols, 0), grads)

    @pl.when(step == 0)
    def _():
        acc[...] = part

    @pl.when(step > 0)
    def _():
        acc[...] += part

    @pl.when(step == pl.num_programs(0) - 1)
    def _():
        half = HD // 2
        for c in range(2):
            for j in range(tiles):
                weight[c, j] = acc[
                    c * half : (c + 1) * half, j * LANES : (j + 1) * LANES
                ].astype(BF)


def project_body(gathered, w_out, packed):
    samples, _, width = gathered.shape
    grads = gathered[:, :LANES, :].reshape(samples * LANES, width)
    part = nt(grads, w_out[...])
    for s in range(samples):
        packed[s] = pack(part[s * LANES : (s + 1) * LANES]).astype(BF)


def attention_body(
    probs, packed, attn_out, queries, keys, values, behind, ahead,
    d_queries, own, to_behind, to_ahead,
):
    rows = queries.shape[0]
    for h in range(HEADS):
        cols = slice(h * HD, (h + 1) * HD)
        grad = unpack(packed[h])
        delta = jnp.sum(
            grad.astype(F32) * attn_out[:, cols].astype(F32), axis=1, keepdims=True
        )
        value_win = jnp.concatenate(
            [behind[rows : 2 * rows, cols], values[:, cols], ahead[rows : 2 * rows, cols]], 0
        )
        key_win = jnp.concatenate([behind[0:rows, cols], keys[:, cols], ahead[0:rows, cols]], 0)
        prob = probs[h]
        dprobs = nt(grad, value_win)
        dscores = (prob * (dprobs - delta) * SCALE).astype(BF)
        d_queries[:, cols] = nn(dscores, key_win).astype(BF)
        for which, (left, right) in enumerate(
            ((dscores, queries[:, cols]), (prob.astype(BF), grad))
        ):
            win = tn(left, right)
            to_behind[which, :, cols] = win[:rows].astype(BF)
            own[which, :, cols] = win[rows : 2 * rows]
            to_ahead[which, :, cols] = win[2 * rows :].astype(BF)


def finish_body(own, from_behind, from_ahead, d_keys, d_values):
    for which, out in enumerate((d_keys, d_values)):
        out[...] = (
            own[which] + from_behind[which].astype(F32) + from_ahead[which].astype(F32)
        ).astype(BF)


def vmem():
    return pl.BlockSpec(memory_space=pltpu.VMEM)


def smem():
    return pl.BlockSpec(memory_space=pltpu.SMEM)


def hbm():
    return pl.BlockSpec(memory_space=pltpu.HBM)


PARAMS = pltpu.CompilerParams(vmem_limit_bytes=48 << 20)


def call(body, outs, specs):
    return pl.pallas_call(
        body,
        out_shape=tuple(jax.ShapeDtypeStruct(shape, dtype) for shape, dtype in outs),
        in_specs=specs,
        out_specs=tuple(vmem() for _ in outs),
        compiler_params=PARAMS,
    )


def shift(value, by):
    length = lax.axis_size(REGION)
    return lax.ppermute(value, REGION, [(i, (i + by) % length) for i in range(length)])


def spread_out(value, ways):
    return jnp.broadcast_to(value[None], (ways,) + value.shape)


def local(queries, keys, values, attn_out, d_out, w_out, adjacency, counts):
    queries, keys, values, attn_out, d_out = (
        a[0] for a in (queries, keys, values, attn_out, d_out)
    )
    rows, hw = queries.shape
    width = d_out.shape[1]
    samples = lax.axis_size(DP)
    sent = (samples, rows + 8, width)
    spread, halo = pl.pallas_call(
        prepare_body,
        out_shape=(
            jax.ShapeDtypeStruct(sent, BF),
            jax.ShapeDtypeStruct((2 * rows + 8, hw), BF),
        ),
        in_specs=[smem()] + [hbm()] * 4,
        out_specs=(hbm(), hbm()),
        scratch_shapes=[
            pltpu.VMEM((rows, width), BF),
            pltpu.VMEM((rows, hw), BF),
            pltpu.VMEM(sent, BF),
            pltpu.VMEM((8, hw), BF),
            pltpu.SemaphoreType.DMA((2,)),
            pltpu.SemaphoreType.DMA((samples,)),
            pltpu.SemaphoreType.DMA((3,)),
        ],
        compiler_params=PARAMS,
    )(counts, d_out, attn_out, keys, values)
    gathered = lax.all_to_all(spread, DP, 0, 0)
    behind = shift(halo, 1)
    ahead = shift(halo, -1)
    (probs,) = call(
        probs_body,
        [((HEADS, rows, 3 * rows), F32)],
        [smem(), smem(), vmem(), vmem(), vmem(), vmem()],
    )(counts, adjacency[0], queries, keys, behind, ahead)
    gathered, probs = lax.optimization_barrier((gathered, probs))

    group = 2
    steps = samples // group
    halves = (2, width // LANES, HD // 2, LANES)
    rows_in = pl.BlockSpec((group, rows + 8, width), lambda i: (i, 0, 0))
    weight = pl.pallas_call(
        weight_body,
        out_shape=jax.ShapeDtypeStruct(halves, BF),
        grid=(steps,),
        in_specs=[rows_in],
        out_specs=pl.BlockSpec(halves, lambda i: (0, 0, 0, 0)),
        scratch_shapes=[pltpu.VMEM((HD, width), F32)],
        compiler_params=PARAMS,
    )(gathered)
    ways = lax.axis_size("y")
    flat = halves[1] * halves[2]
    pair = lax.all_to_all(weight, "core", 0, 0)
    half = jnp.sum(pair.astype(F32), axis=0).astype(BF)
    gathered, half = lax.optimization_barrier((gathered, half))
    packed = pl.pallas_call(
        project_body,
        out_shape=jax.ShapeDtypeStruct((samples, HD, LANES), BF),
        grid=(steps,),
        in_specs=[rows_in, pl.BlockSpec((HD, width), lambda i: (0, 0))],
        out_specs=pl.BlockSpec((group, HD, LANES), lambda i: (i, 0, 0)),
        compiler_params=PARAMS,
    )(gathered, w_out)
    terms = lax.all_to_all(half.reshape(ways, flat // ways, LANES), "y", 0, 0)
    terms, packed = lax.optimization_barrier((terms, packed))
    packed = lax.all_to_all(packed, DP, 0, 0)
    terms = jnp.sum(terms.astype(F32), axis=0).astype(BF)
    terms = lax.all_to_all(spread_out(terms, lax.axis_size("z_hi")), "z_hi", 0, 0)
    total = jnp.sum(terms.astype(F32), axis=0).astype(BF)
    total = lax.all_to_all(spread_out(total, ways), "y", 0, 0).reshape(flat, LANES)
    both = lax.all_to_all(spread_out(total, 2), "core", 0, 0)
    d_weight = both.reshape(halves).transpose(0, 2, 1, 3).reshape(HD, width)

    pairs = (2, rows, hw)
    d_queries, own, to_behind, to_ahead = call(
        attention_body,
        [((rows, hw), BF), (pairs, F32), (pairs, BF), (pairs, BF)],
        [vmem()] * 8,
    )(probs, packed, attn_out, queries, keys, values, behind, ahead)
    d_keys, d_values = call(
        finish_body, [((rows, hw), BF), ((rows, hw), BF)], [vmem()] * 3
    )(own, shift(to_ahead, 1), shift(to_behind, -1))
    return d_queries[None], d_keys[None], d_values[None], d_weight


def solution(mesh):
    parts = Mesh(mesh.devices.reshape(2, 4, 8, 4, 2), DP + REGION)
    rows = P(DP, REGION, None)
    return jax.shard_map(
        local,
        mesh=parts,
        in_specs=(rows, rows, rows, rows, rows, P(DP, None), P(REGION, None, None), P(REGION)),
        out_specs=(rows, rows, rows, P(DP, None)),
        check_vma=False,
    )
```

```python
import math

import jax
import jax.numpy as jnp
from jax import lax
from jax.experimental import pallas as pl
from jax.experimental.pallas import tpu as pltpu
from jax.sharding import Mesh
from jax.sharding import PartitionSpec as P

HEADS = 8
HD = 160
BLK = 4
DP = ("z_lo", "x")
REGION = ("y", "z_hi", "core")
BF = jnp.bfloat16
F32 = jnp.float32
LANES = 128
SCALE = 1.0 / math.sqrt(HD)


def nn(a, b):
    return lax.dot_general(a, b, (((1,), (0,)), ((), ())), preferred_element_type=F32)


def nt(a, b):
    return lax.dot_general(a, b, (((1,), (1,)), ((), ())), preferred_element_type=F32)


def tn(a, b):
    return lax.dot_general(a, b, (((0,), (0,)), ((), ())), preferred_element_type=F32)


def prepare_body(
    counts, d_out, attn_out, keys, values, spread, grads, halo,
    grads_in, tail, sem_in, sem_attn, sem_out, sem_halo,
):
    rows, width = d_out.shape
    samples, _, part = spread.shape
    load = pltpu.make_async_copy(d_out, grads_in, sem_in.at[0])
    load.start()
    copies = []
    down = width // part
    for s in range(samples):
        half = pl.ds(s // down * part, part)
        copies.append(
            pltpu.make_async_copy(
                attn_out.at[:, half], spread.at[s, pl.ds(0, rows)], sem_attn.at[s]
            )
        )
    tail[...] = jnp.full(tail.shape, counts[0].astype(F32), F32).astype(BF)
    copies += [
        pltpu.make_async_copy(keys, halo.at[pl.ds(0, rows)], sem_halo.at[0]),
        pltpu.make_async_copy(values, halo.at[pl.ds(rows, rows)], sem_halo.at[1]),
        pltpu.make_async_copy(tail, halo.at[pl.ds(2 * rows, 8)], sem_halo.at[2]),
    ]
    for copy in copies:
        copy.start()
    load.wait()
    live = lax.broadcasted_iota(jnp.int32, (rows, 1), 0) // (rows // BLK) < counts[0]
    grads_in[...] = jnp.where(live, grads_in[...], jnp.zeros((), BF))
    stores = [pltpu.make_async_copy(grads_in, grads, sem_in.at[1])]
    for s in range(samples):
        quarter = pl.ds(s % down * part, part)
        stores.append(
            pltpu.make_async_copy(
                grads_in.at[:, quarter], spread.at[s, pl.ds(rows, rows)], sem_out.at[s]
            )
        )
    for copy in stores:
        copy.start()
    for copy in copies + stores:
        copy.wait()


def probs_body(counts, adjacency, queries, keys, behind, ahead, probs):
    rows = queries.shape[0]
    block = rows // BLK
    width = 3 * rows
    lane = lax.broadcasted_iota(jnp.int32, (1, width), 1)
    key_block = lane // block
    count = jnp.concatenate(
        [
            behind[2 * rows : 2 * rows + 1, :rows].astype(F32),
            jnp.full((1, rows), counts[0].astype(F32), F32),
            ahead[2 * rows : 2 * rows + 1, :rows].astype(F32),
        ],
        1,
    )
    live = (key_block % BLK).astype(F32) < count
    bias = []
    for a in range(BLK):
        seen = jnp.zeros((1, width), jnp.int32)
        for j in range(3 * BLK):
            seen = jnp.where(key_block == j, adjacency[a, j], seen)
        ok = jnp.logical_or(jnp.logical_and(seen == 1, live), key_block == BLK + a)
        bias.append(jnp.broadcast_to(jnp.where(ok, 1.0, 0.0), (block, width)))
    allowed = jnp.concatenate(bias, 0) > 0.5
    for h in range(HEADS):
        cols = slice(h * HD, (h + 1) * HD)
        window = jnp.concatenate([behind[0:rows, cols], keys[:, cols], ahead[0:rows, cols]], 0)
        scores = jnp.where(allowed, nt(queries[:, cols], window) * SCALE, -1e30)
        maxima = jnp.max(scores, axis=1, keepdims=True)
        terms = jnp.where(allowed, jnp.exp(scores - maxima), 0.0)
        probs[h] = terms / jnp.sum(terms, axis=1, keepdims=True)


def weight_body(gathered, weight, acc):
    step = pl.program_id(0)
    samples, both, part = gathered.shape
    cores, chips, heads, share, _ = weight.shape
    rows = both // 2
    left = gathered[:, :rows, :].reshape(samples * rows, part)
    right = gathered[:, rows:, :].reshape(samples * rows, part)
    term = tn(left, right)

    @pl.when(step == 0)
    def _():
        acc[...] = term

    @pl.when(step > 0)
    def _():
        acc[...] += term

    @pl.when(step == pl.num_programs(0) - 1)
    def _():
        half = HD // cores
        tiles = part // LANES
        for c in range(cores):
            for h in range(heads):
                first = h * HD + c * half
                pieces = [
                    acc[first : first + half, j * LANES : (j + 1) * LANES] for j in range(tiles)
                ]
                pieces.append(jnp.zeros((chips * share - tiles * half, LANES), F32))
                flat = jnp.concatenate(pieces, 0).reshape(chips, share, LANES)
                for m in range(chips):
                    weight[c, m, h] = flat[m].astype(BF)


def assemble_body(both, d_weight):
    cores, chips, quarters, _, _ = both.shape
    half = HD // cores
    part = d_weight.shape[1] // quarters
    for c in range(cores):
        for q in range(quarters):
            flat = jnp.concatenate([both[c, m, q].astype(F32) for m in range(chips)], 0)
            for j in range(part // LANES):
                first = q * part + j * LANES
                d_weight[c * half : (c + 1) * half, first : first + LANES] = flat[
                    j * half : (j + 1) * half
                ].astype(BF)


def attention_body(
    w_all, probs, grads, attn_out, queries, keys, values, behind, ahead,
    d_queries, own, to_behind, to_ahead, w_in, sem,
):
    rows = queries.shape[0]
    loads = [pltpu.make_async_copy(w_all.at[h], w_in.at[h], sem.at[h]) for h in range(HEADS)]
    for load in loads:
        load.start()
    for h in range(HEADS):
        cols = slice(h * HD, (h + 1) * HD)
        loads[h].wait()
        grad = nt(grads[...], w_in[h]).astype(BF)
        delta = jnp.sum(
            grad.astype(F32) * attn_out[:, cols].astype(F32), axis=1, keepdims=True
        )
        value_win = jnp.concatenate(
            [behind[rows : 2 * rows, cols], values[:, cols], ahead[rows : 2 * rows, cols]], 0
        )
        key_win = jnp.concatenate([behind[0:rows, cols], keys[:, cols], ahead[0:rows, cols]], 0)
        prob = probs[h]
        dprobs = nt(grad, value_win)
        dscores = (prob * (dprobs - delta) * SCALE).astype(BF)
        d_queries[:, cols] = nn(dscores, key_win).astype(BF)
        for which, (left, right) in enumerate(
            ((dscores, queries[:, cols]), (prob.astype(BF), grad))
        ):
            win = tn(left, right)
            to_behind[which, :, cols] = win[:rows].astype(BF)
            own[which, :, cols] = win[rows : 2 * rows]
            to_ahead[which, :, cols] = win[2 * rows :].astype(BF)


def finish_body(own, from_behind, from_ahead, d_keys, d_values):
    for which, out in enumerate((d_keys, d_values)):
        out[...] = (
            own[which] + from_behind[which].astype(F32) + from_ahead[which].astype(F32)
        ).astype(BF)


def vmem():
    return pl.BlockSpec(memory_space=pltpu.VMEM)


def smem():
    return pl.BlockSpec(memory_space=pltpu.SMEM)


def hbm():
    return pl.BlockSpec(memory_space=pltpu.HBM)


def in_hbm(value):
    return pltpu.with_memory_space_constraint(value, pltpu.HBM)


PARAMS = pltpu.CompilerParams(vmem_limit_bytes=28 << 20)


def call(body, outs, specs, scratch=()):
    return pl.pallas_call(
        body,
        out_shape=tuple(jax.ShapeDtypeStruct(shape, dtype) for shape, dtype in outs),
        in_specs=specs,
        out_specs=tuple(vmem() for _ in outs),
        scratch_shapes=scratch,
        compiler_params=PARAMS,
    )


def shift(value, by):
    length = lax.axis_size(REGION)
    return lax.ppermute(value, REGION, [(i, (i + by) % length) for i in range(length)])


def spread_out(value, ways):
    return jnp.broadcast_to(value[None], (ways,) + value.shape)


def local(queries, keys, values, attn_out, d_out, w_out, adjacency, counts):
    queries, keys, values, attn_out, d_out = (
        a[0] for a in (queries, keys, values, attn_out, d_out)
    )
    rows, hw = queries.shape
    width = d_out.shape[1]
    samples = lax.axis_size(DP)
    cores = lax.axis_size("core")
    chips = lax.axis_size("y")
    down = lax.axis_size("x")
    across = lax.axis_size("z_hi")
    part = width // down
    half = HD // cores

    w_half = lax.dynamic_slice_in_dim(w_out, lax.axis_index("core") * half, half, 0)
    w_all = lax.all_gather(w_half, DP + ("core",), axis=0, tiled=True)

    sent = (samples, 2 * rows, part)
    spread, grads, halo = pl.pallas_call(
        prepare_body,
        out_shape=(
            pltpu.HBM(sent, BF),
            pltpu.HBM((rows, width), BF),
            pltpu.HBM((2 * rows + 8, hw), BF),
        ),
        in_specs=[smem()] + [hbm()] * 4,
        out_specs=(hbm(), hbm(), hbm()),
        scratch_shapes=[
            pltpu.VMEM((rows, width), BF),
            pltpu.VMEM((8, hw), BF),
            pltpu.SemaphoreType.DMA((2,)),
            pltpu.SemaphoreType.DMA((samples,)),
            pltpu.SemaphoreType.DMA((samples,)),
            pltpu.SemaphoreType.DMA((3,)),
        ],
        compiler_params=PARAMS,
    )(counts, in_hbm(d_out), in_hbm(attn_out), in_hbm(keys), in_hbm(values))
    gathered = lax.all_to_all(spread, DP, 0, 0)
    behind = shift(halo, 1)
    ahead = shift(halo, -1)

    group = 2
    share = -(-(half * part // LANES) // (8 * chips)) * 8
    pieces = (cores, chips, down, share, LANES)
    weight = pl.pallas_call(
        weight_body,
        out_shape=jax.ShapeDtypeStruct(pieces, BF),
        grid=(samples // group,),
        in_specs=[pl.BlockSpec((group, 2 * rows, part), lambda i: (i, 0, 0))],
        out_specs=pl.BlockSpec(pieces, lambda i: (0, 0, 0, 0, 0)),
        scratch_shapes=[pltpu.VMEM((part, part), F32)],
        compiler_params=PARAMS,
    )(gathered)

    pair = lax.all_to_all(weight, "core", 0, 0)
    terms = jnp.sum(pair.astype(F32), axis=0).astype(BF)
    terms, behind, ahead = lax.optimization_barrier((terms, behind, ahead))
    (probs,) = call(
        probs_body,
        [((HEADS, rows, 3 * rows), F32)],
        [smem(), smem(), vmem(), vmem(), vmem(), vmem()],
    )(counts, adjacency[0], queries, keys, behind, ahead)
    terms = lax.all_to_all(terms, "y", 0, 0)
    terms, probs = lax.optimization_barrier((terms, probs))
    terms = jnp.sum(terms.astype(F32), axis=0).astype(BF)
    terms = jnp.broadcast_to(terms[:, None], (down, across, share, LANES))
    terms = terms.reshape(down * across, share, LANES)
    terms = lax.all_to_all(terms, ("x", "z_hi"), 0, 0).reshape(down, across, share, LANES)
    total = jnp.sum(terms.astype(F32), axis=1).astype(BF)
    total = lax.all_to_all(spread_out(total, chips), "y", 0, 0)
    both = lax.all_to_all(spread_out(total, cores), "core", 0, 0)
    (d_weight,) = call(assemble_body, [((HD, width), BF)], [vmem()])(both)

    pairs = (2, rows, hw)
    d_queries, own, to_behind, to_ahead = call(
        attention_body,
        [((rows, hw), BF), (pairs, F32), (pairs, BF), (pairs, BF)],
        [hbm()] + [vmem()] * 8,
        [pltpu.VMEM((HEADS, HD, width), BF), pltpu.SemaphoreType.DMA((HEADS,))],
    )(
        in_hbm(w_all.reshape(HEADS, HD, width)),
        probs, grads, attn_out, queries, keys, values, behind, ahead,
    )
    d_keys, d_values = call(
        finish_body, [((rows, hw), BF), ((rows, hw), BF)], [vmem()] * 3
    )(own, shift(to_ahead, 1), shift(to_behind, -1))
    return d_queries[None], d_keys[None], d_values[None], d_weight


def solution(mesh):
    parts = Mesh(mesh.devices.reshape(2, 4, 8, 4, 2), DP + REGION)
    rows = P(DP, REGION, None)
    return jax.shard_map(
        local,
        mesh=parts,
        in_specs=(rows, rows, rows, rows, rows, P(DP, None), P(REGION, None, None), P(REGION)),
        out_specs=(rows, rows, rows, P(DP, None)),
        check_vma=False,
    )
```

```python
import math

import jax
import jax.numpy as jnp
from jax import lax
from jax.experimental import pallas as pl
from jax.experimental.pallas import tpu as pltpu
from jax.sharding import Mesh
from jax.sharding import PartitionSpec as P

HEADS = 8
HD = 160
BLK = 4
DP = ("z_lo", "x")
REGION = ("y", "z_hi", "core")
BF = jnp.bfloat16
F32 = jnp.float32
LANES = 128
SCALE = 1.0 / math.sqrt(HD)


def nn(a, b):
    return lax.dot_general(a, b, (((1,), (0,)), ((), ())), preferred_element_type=F32)


def nt(a, b):
    return lax.dot_general(a, b, (((1,), (1,)), ((), ())), preferred_element_type=F32)


def tn(a, b):
    return lax.dot_general(a, b, (((0,), (0,)), ((), ())), preferred_element_type=F32)


def prepare_body(
    counts, core, d_out, attn_out, keys, values, w_out, w_half, spread, grads, halo,
    w_in, grads_in, attn_in, tail, halo_in, sem_in, sem_attn, sem_out, sem_halo,
):
    rows, width = d_out.shape
    samples, _, part = spread.shape
    down = width // part
    half_rows = w_half.shape[0]
    first_row = pl.multiple_of(core[0] * half_rows, half_rows)
    w_load = pltpu.make_async_copy(w_out.at[pl.ds(first_row, half_rows)], w_in, sem_in.at[4])
    w_load.start()
    loads = [
        pltpu.make_async_copy(d_out, grads_in, sem_in.at[0]),
        pltpu.make_async_copy(attn_out, attn_in, sem_in.at[1]),
        pltpu.make_async_copy(keys, halo_in.at[pl.ds(0, rows)], sem_in.at[2]),
        pltpu.make_async_copy(values, halo_in.at[pl.ds(rows, rows)], sem_in.at[3]),
    ]
    for load in loads:
        load.start()
    tail[...] = jnp.full(tail.shape, counts[0].astype(F32), F32).astype(BF)
    stores = [pltpu.make_async_copy(tail, halo.at[pl.ds(2 * rows, 8)], sem_halo.at[1])]
    live = lax.broadcasted_iota(jnp.int32, (rows, 1), 0) // (rows // BLK) < counts[0]
    w_load.wait()
    stores.append(pltpu.make_async_copy(w_in, w_half, sem_halo.at[3]))
    loads[0].wait()
    grads_in[...] = jnp.where(live, grads_in[...], jnp.zeros((), BF))
    for s in range(samples):
        quarter = pl.ds(s % down * part, part)
        stores.append(
            pltpu.make_async_copy(
                grads_in.at[:, quarter], spread.at[s, pl.ds(rows, rows)], sem_out.at[s]
            )
        )
    stores.append(pltpu.make_async_copy(grads_in, grads, sem_halo.at[2]))
    for store in stores:
        store.start()
    loads[1].wait()
    for s in range(samples):
        half = pl.ds(s // down * part, part)
        stores.append(
            pltpu.make_async_copy(
                attn_in.at[:, half], spread.at[s, pl.ds(0, rows)], sem_attn.at[s]
            )
        )
        stores[-1].start()
    loads[2].wait()
    loads[3].wait()
    stores.append(
        pltpu.make_async_copy(halo_in, halo.at[pl.ds(0, 2 * rows)], sem_halo.at[0])
    )
    stores[-1].start()
    for store in stores:
        store.wait()


def allowed_pairs(counts, adjacency, behind, ahead, rows):
    block = rows // BLK
    width = 3 * rows
    key_block = lax.broadcasted_iota(jnp.int32, (1, width), 1) // block
    count = jnp.concatenate(
        [
            behind[2 * rows : 2 * rows + 1, :rows].astype(F32),
            jnp.full((1, rows), counts[0].astype(F32), F32),
            ahead[2 * rows : 2 * rows + 1, :rows].astype(F32),
        ],
        1,
    )
    live = (key_block % BLK).astype(F32) < count
    bias = []
    for a in range(BLK):
        seen = jnp.zeros((1, width), jnp.int32)
        for j in range(3 * BLK):
            seen = jnp.where(key_block == j, adjacency[a, j], seen)
        ok = jnp.logical_or(jnp.logical_and(seen == 1, live), key_block == BLK + a)
        bias.append(jnp.broadcast_to(jnp.where(ok, 1.0, 0.0), (block, width)))
    return jnp.concatenate(bias, 0) > 0.5


def weight_body(gathered, weight, acc):
    step = pl.program_id(0)
    samples, both, part = gathered.shape
    cores, chips, heads, share, _ = weight.shape
    rows = both // 2
    left = gathered[:, :rows, :].reshape(samples * rows, part)
    right = gathered[:, rows:, :].reshape(samples * rows, part)
    term = tn(left, right)

    @pl.when(step == 0)
    def _():
        acc[...] = term

    @pl.when(step > 0)
    def _():
        acc[...] += term

    @pl.when(step == pl.num_programs(0) - 1)
    def _():
        half = HD // cores
        tiles = part // LANES
        for c in range(cores):
            for h in range(heads):
                first = h * HD + c * half
                pieces = [
                    acc[first : first + half, j * LANES : (j + 1) * LANES] for j in range(tiles)
                ]
                pieces.append(jnp.zeros((chips * share - tiles * half, LANES), F32))
                flat = jnp.concatenate(pieces, 0).reshape(chips, share, LANES)
                for m in range(chips):
                    weight[c, m, h] = flat[m].astype(BF)


def assemble_body(both, d_weight):
    cores, chips, quarters, _, _ = both.shape
    half = HD // cores
    part = d_weight.shape[1] // quarters
    for c in range(cores):
        for q in range(quarters):
            flat = jnp.concatenate([both[c, m, q].astype(F32) for m in range(chips)], 0)
            for j in range(part // LANES):
                first = q * part + j * LANES
                d_weight[c * half : (c + 1) * half, first : first + LANES] = flat[
                    j * half : (j + 1) * half
                ].astype(BF)


def attention_body(counts, adjacency, *refs):
    sources, rest = refs[:8], refs[8:]
    targets, rest = rest[:4], rest[4:]
    arrays, rest = rest[:8], rest[8:]
    results, (sem_w, sem_in, sem_out) = rest[:4], rest[4:]
    w_all, *sources = sources
    w_in, *arrays = arrays
    queries, keys, behind, ahead, grads, attn_out, values = arrays
    d_queries, own, to_behind, to_ahead = results
    rows = queries.shape[0]
    loads = [
        pltpu.make_async_copy(source, array, sem_in.at[i])
        for i, (source, array) in enumerate(zip(sources, arrays))
    ]
    w_loads = [pltpu.make_async_copy(w_all.at[h], w_in.at[h], sem_w.at[h]) for h in range(HEADS)]
    for load in loads + w_loads:
        load.start()
    for load in loads:
        load.wait()
    allowed = allowed_pairs(counts, adjacency, behind, ahead, rows)
    for h in range(HEADS):
        cols = slice(h * HD, (h + 1) * HD)
        key_win = jnp.concatenate([behind[0:rows, cols], keys[:, cols], ahead[0:rows, cols]], 0)
        query = queries[:, cols]
        scores = jnp.where(allowed, nt(query, key_win) * SCALE, -1e30)
        terms = jnp.exp(scores - jnp.max(scores, axis=1, keepdims=True))
        terms = jnp.where(allowed, terms, 0.0)
        prob = terms / jnp.sum(terms, axis=1, keepdims=True)
        w_loads[h].wait()
        grad = nt(grads[...], w_in[h]).astype(BF)
        delta = jnp.sum(
            grad.astype(F32) * attn_out[:, cols].astype(F32), axis=1, keepdims=True
        )
        value_win = jnp.concatenate(
            [behind[rows : 2 * rows, cols], values[:, cols], ahead[rows : 2 * rows, cols]], 0
        )
        dprobs = nt(grad, value_win)
        dscores = (prob * (dprobs - delta) * SCALE).astype(BF)
        d_queries[:, cols] = nn(dscores, key_win).astype(BF)
        for which, (left, right) in enumerate(((dscores, query), (prob.astype(BF), grad))):
            win = tn(left, right)
            to_behind[which, :, cols] = win[:rows].astype(BF)
            own[which, :, cols] = win[rows : 2 * rows]
            to_ahead[which, :, cols] = win[2 * rows :].astype(BF)
    stores = [
        pltpu.make_async_copy(result, target, sem_out.at[i])
        for i, (result, target) in enumerate(zip(results, targets))
    ]
    for store in stores:
        store.start()
    for store in stores:
        store.wait()


def finish_body(own, from_behind, from_ahead, d_keys, d_values):
    for which, out in enumerate((d_keys, d_values)):
        out[...] = (
            own[which] + from_behind[which].astype(F32) + from_ahead[which].astype(F32)
        ).astype(BF)


def vmem():
    return pl.BlockSpec(memory_space=pltpu.VMEM)


def smem():
    return pl.BlockSpec(memory_space=pltpu.SMEM)


def hbm():
    return pl.BlockSpec(memory_space=pltpu.HBM)


def in_hbm(value):
    return pltpu.with_memory_space_constraint(value, pltpu.HBM)


PARAMS = pltpu.CompilerParams(vmem_limit_bytes=20 << 20)


def call(body, outs, specs, scratch=()):
    return pl.pallas_call(
        body,
        out_shape=tuple(jax.ShapeDtypeStruct(shape, dtype) for shape, dtype in outs),
        in_specs=specs,
        out_specs=tuple(vmem() for _ in outs),
        scratch_shapes=scratch,
        compiler_params=PARAMS,
    )


def shift(value, by):
    length = lax.axis_size(REGION)
    return lax.ppermute(value, REGION, [(i, (i + by) % length) for i in range(length)])


def spread_out(value, ways):
    return jnp.broadcast_to(value[None], (ways,) + value.shape)


def local(queries, keys, values, attn_out, d_out, w_out, adjacency, counts):
    queries, keys, values, attn_out, d_out = (
        a[0] for a in (queries, keys, values, attn_out, d_out)
    )
    rows, hw = queries.shape
    width = d_out.shape[1]
    samples = lax.axis_size(DP)
    cores = lax.axis_size("core")
    chips = lax.axis_size("y")
    down = lax.axis_size("x")
    across = lax.axis_size("z_hi")
    part = width // down
    half = HD // cores

    core = lax.axis_index("core").reshape(1)
    w_half, spread, grads, halo = pl.pallas_call(
        prepare_body,
        out_shape=(
            pltpu.HBM((half, width), BF),
            pltpu.HBM((samples, 2 * rows, part), BF),
            pltpu.HBM((rows, width), BF),
            pltpu.HBM((2 * rows + 8, hw), BF),
        ),
        in_specs=[smem()] * 2 + [hbm()] * 5,
        out_specs=(hbm(),) * 4,
        scratch_shapes=[
            pltpu.VMEM((half, width), BF),
            pltpu.VMEM((rows, width), BF),
            pltpu.VMEM((rows, hw), BF),
            pltpu.VMEM((8, hw), BF),
            pltpu.VMEM((2 * rows, hw), BF),
            pltpu.SemaphoreType.DMA((5,)),
            pltpu.SemaphoreType.DMA((samples,)),
            pltpu.SemaphoreType.DMA((samples,)),
            pltpu.SemaphoreType.DMA((4,)),
        ],
        compiler_params=PARAMS,
    )(counts, core, *(in_hbm(a) for a in (d_out, attn_out, keys, values, w_out)))
    w_all = lax.all_gather(w_half, DP + ("core",), axis=0, tiled=True)

    gathered = lax.all_to_all(spread, DP, 0, 0)

    group = 2
    share = -(-(half * part // LANES) // (8 * chips)) * 8
    pieces = (cores, chips, down, share, LANES)
    weight = pl.pallas_call(
        weight_body,
        out_shape=jax.ShapeDtypeStruct(pieces, BF),
        grid=(samples // group,),
        in_specs=[pl.BlockSpec((group, 2 * rows, part), lambda i: (i, 0, 0))],
        out_specs=pl.BlockSpec(pieces, lambda i: (0, 0, 0, 0, 0)),
        scratch_shapes=[pltpu.VMEM((part, part), F32)],
        compiler_params=PARAMS,
    )(gathered)

    pair = lax.all_to_all(weight, "core", 0, 0)
    terms = jnp.sum(pair.astype(F32), axis=0).astype(BF)
    terms, halo = lax.optimization_barrier((terms, halo))
    behind = shift(halo, 1)
    ahead = shift(halo, -1)
    terms = lax.all_to_all(terms, "y", 0, 0)
    terms = jnp.sum(terms.astype(F32), axis=0).astype(BF)
    terms = jnp.broadcast_to(terms[:, None], (down, across, share, LANES))
    terms = terms.reshape(down * across, share, LANES)
    terms, grads = lax.optimization_barrier((terms, grads))
    operands = (
        w_all.reshape(HEADS, HD, width), queries, keys, behind, ahead, grads, attn_out, values,
    )
    pairs = (2, rows, hw)
    results = (((rows, hw), BF), (pairs, F32), (pairs, BF), (pairs, BF))
    d_queries, own, to_behind, to_ahead = pl.pallas_call(
        attention_body,
        out_shape=tuple(pltpu.HBM(shape, dtype) for shape, dtype in results),
        in_specs=[smem()] * 2 + [hbm()] * len(operands),
        out_specs=(hbm(),) * len(results),
        scratch_shapes=[pltpu.VMEM(a.shape, a.dtype) for a in operands]
        + [pltpu.VMEM(shape, dtype) for shape, dtype in results]
        + [
            pltpu.SemaphoreType.DMA((HEADS,)),
            pltpu.SemaphoreType.DMA((len(operands) - 1,)),
            pltpu.SemaphoreType.DMA((len(results),)),
        ],
        compiler_params=PARAMS,
    )(counts, adjacency[0], *(in_hbm(a) for a in operands))
    terms = lax.all_to_all(terms, ("x", "z_hi"), 0, 0).reshape(down, across, share, LANES)
    terms, own = lax.optimization_barrier((terms, own))
    total = jnp.sum(terms.astype(F32), axis=1).astype(BF)
    total = lax.all_to_all(spread_out(total, chips), "y", 0, 0)
    both = lax.all_to_all(spread_out(total, cores), "core", 0, 0)
    (d_weight,) = call(assemble_body, [((HD, width), BF)], [vmem()])(both)

    d_keys, d_values = call(
        finish_body, [((rows, hw), BF), ((rows, hw), BF)], [vmem()] * 3
    )(own, shift(to_ahead, 1), shift(to_behind, -1))
    return d_queries[None], d_keys[None], d_values[None], d_weight


def solution(mesh):
    parts = Mesh(mesh.devices.reshape(2, 4, 8, 4, 2), DP + REGION)
    rows = P(DP, REGION, None)
    return jax.shard_map(
        local,
        mesh=parts,
        in_specs=(rows, rows, rows, rows, rows, P(DP, None), P(REGION, None, None), P(REGION)),
        out_specs=(rows, rows, rows, P(DP, None)),
        check_vma=False,
    )
```

```python
import math

import jax
import jax.numpy as jnp
from jax import lax
from jax.experimental import pallas as pl
from jax.experimental.pallas import tpu as pltpu
from jax.sharding import Mesh
from jax.sharding import PartitionSpec as P

HEADS = 8
HD = 160
BLK = 4
DP = ("z_lo", "x")
REGION = ("y", "z_hi", "core")
BF = jnp.bfloat16
F32 = jnp.float32
LANES = 128
SCALE = 1.0 / math.sqrt(HD)


def nn(a, b):
    return lax.dot_general(a, b, (((1,), (0,)), ((), ())), preferred_element_type=F32)


def nt(a, b):
    return lax.dot_general(a, b, (((1,), (1,)), ((), ())), preferred_element_type=F32)


def tn(a, b):
    return lax.dot_general(a, b, (((0,), (0,)), ((), ())), preferred_element_type=F32)


def prepare_body(
    counts, core, d_out, attn_out, keys, values, w_out, w_half, spread, grads, halo,
    w_in, grads_in, attn_in, tail, halo_in, sem_in, sem_attn, sem_out, sem_halo,
):
    rows, width = d_out.shape
    samples, _, part = spread.shape
    down = width // part
    half_rows = w_half.shape[0]
    first_row = pl.multiple_of(core[0] * half_rows, half_rows)
    w_load = pltpu.make_async_copy(w_out.at[pl.ds(first_row, half_rows)], w_in, sem_in.at[4])
    w_load.start()
    loads = [
        pltpu.make_async_copy(d_out, grads_in, sem_in.at[0]),
        pltpu.make_async_copy(attn_out, attn_in, sem_in.at[1]),
        pltpu.make_async_copy(keys, halo_in.at[pl.ds(0, rows)], sem_in.at[2]),
        pltpu.make_async_copy(values, halo_in.at[pl.ds(rows, rows)], sem_in.at[3]),
    ]
    for load in loads:
        load.start()
    tail[...] = jnp.full(tail.shape, counts[0].astype(F32), F32).astype(BF)
    stores = [pltpu.make_async_copy(tail, halo.at[pl.ds(2 * rows, 8)], sem_halo.at[1])]
    live = lax.broadcasted_iota(jnp.int32, (rows, 1), 0) // (rows // BLK) < counts[0]
    w_load.wait()
    stores.append(pltpu.make_async_copy(w_in, w_half, sem_halo.at[3]))
    loads[0].wait()
    grads_in[...] = jnp.where(live, grads_in[...], jnp.zeros((), BF))
    for s in range(samples):
        quarter = pl.ds(s % down * part, part)
        stores.append(
            pltpu.make_async_copy(
                grads_in.at[:, quarter], spread.at[s, pl.ds(rows, rows)], sem_out.at[s]
            )
        )
    stores.append(pltpu.make_async_copy(grads_in, grads, sem_halo.at[2]))
    for store in stores:
        store.start()
    loads[1].wait()
    for s in range(samples):
        half = pl.ds(s // down * part, part)
        stores.append(
            pltpu.make_async_copy(
                attn_in.at[:, half], spread.at[s, pl.ds(0, rows)], sem_attn.at[s]
            )
        )
        stores[-1].start()
    loads[2].wait()
    loads[3].wait()
    stores.append(
        pltpu.make_async_copy(halo_in, halo.at[pl.ds(0, 2 * rows)], sem_halo.at[0])
    )
    stores[-1].start()
    for store in stores:
        store.wait()


def allowed_pairs(counts, adjacency, behind, ahead, rows):
    block = rows // BLK
    width = 3 * rows
    key_block = lax.broadcasted_iota(jnp.int32, (1, width), 1) // block
    count = jnp.concatenate(
        [
            behind[2 * rows : 2 * rows + 1, :rows].astype(F32),
            jnp.full((1, rows), counts[0].astype(F32), F32),
            ahead[2 * rows : 2 * rows + 1, :rows].astype(F32),
        ],
        1,
    )
    live = (key_block % BLK).astype(F32) < count
    bias = []
    for a in range(BLK):
        seen = jnp.zeros((1, width), jnp.int32)
        for j in range(3 * BLK):
            seen = jnp.where(key_block == j, adjacency[a, j], seen)
        ok = jnp.logical_or(jnp.logical_and(seen == 1, live), key_block == BLK + a)
        bias.append(jnp.broadcast_to(jnp.where(ok, 1.0, 0.0), (block, width)))
    return jnp.concatenate(bias, 0) > 0.5


def weight_body(gathered, weight, acc):
    step = pl.program_id(0)
    samples, both, part = gathered.shape
    cores, chips, heads, share, _ = weight.shape
    rows = both // 2
    left = gathered[:, :rows, :].reshape(samples * rows, part)
    right = gathered[:, rows:, :].reshape(samples * rows, part)
    term = tn(left, right)

    @pl.when(step == 0)
    def _():
        acc[...] = term

    @pl.when(step > 0)
    def _():
        acc[...] += term

    @pl.when(step == pl.num_programs(0) - 1)
    def _():
        half = HD // cores
        tiles = part // LANES
        for c in range(cores):
            for h in range(heads):
                first = h * HD + c * half
                pieces = [
                    acc[first : first + half, j * LANES : (j + 1) * LANES] for j in range(tiles)
                ]
                pieces.append(jnp.zeros((chips * share - tiles * half, LANES), F32))
                flat = jnp.concatenate(pieces, 0).reshape(chips, share, LANES)
                for m in range(chips):
                    weight[c, m, h] = flat[m].astype(BF)


def assemble_body(both, d_weight):
    cores, chips, quarters, _, _ = both.shape
    half = HD // cores
    part = d_weight.shape[1] // quarters
    for c in range(cores):
        for q in range(quarters):
            flat = jnp.concatenate([both[c, m, q].astype(F32) for m in range(chips)], 0)
            for j in range(part // LANES):
                first = q * part + j * LANES
                d_weight[c * half : (c + 1) * half, first : first + LANES] = flat[
                    j * half : (j + 1) * half
                ].astype(BF)


def attention_body(counts, adjacency, *refs):
    sources, rest = refs[:8], refs[8:]
    targets, rest = rest[:4], rest[4:]
    arrays, rest = rest[:8], rest[8:]
    results, (sem_w, sem_in, sem_out) = rest[:4], rest[4:]
    w_all, *sources = sources
    w_in, *arrays = arrays
    queries, keys, behind, ahead, grads, attn_out, values = arrays
    d_queries, own, to_behind, to_ahead = results
    rows = queries.shape[0]
    loads = [
        pltpu.make_async_copy(source, array, sem_in.at[i])
        for i, (source, array) in enumerate(zip(sources, arrays))
    ]
    w_loads = [pltpu.make_async_copy(w_all.at[h], w_in.at[h], sem_w.at[h]) for h in range(HEADS)]
    for load in loads + w_loads:
        load.start()
    for load in loads + w_loads:
        load.wait()
    allowed = allowed_pairs(counts, adjacency, behind, ahead, rows)
    for h in range(HEADS):
        cols = slice(h * HD, (h + 1) * HD)
        key_win = jnp.concatenate([behind[0:rows, cols], keys[:, cols], ahead[0:rows, cols]], 0)
        query = queries[:, cols]
        scores = jnp.where(allowed, nt(query, key_win) * SCALE, -1e30)
        terms = jnp.exp(scores - jnp.max(scores, axis=1, keepdims=True))
        terms = jnp.where(allowed, terms, 0.0)
        prob = terms / jnp.sum(terms, axis=1, keepdims=True)
        grad = nt(grads[...], w_in[h]).astype(BF)
        delta = jnp.sum(
            grad.astype(F32) * attn_out[:, cols].astype(F32), axis=1, keepdims=True
        )
        value_win = jnp.concatenate(
            [behind[rows : 2 * rows, cols], values[:, cols], ahead[rows : 2 * rows, cols]], 0
        )
        dprobs = nt(grad, value_win)
        dscores = (prob * (dprobs - delta) * SCALE).astype(BF)
        d_queries[:, cols] = nn(dscores, key_win).astype(BF)
        for which, (left, right) in enumerate(((dscores, query), (prob.astype(BF), grad))):
            win = tn(left, right)
            to_behind[which, :, cols] = win[:rows].astype(BF)
            own[which, :, cols] = win[rows : 2 * rows]
            to_ahead[which, :, cols] = win[2 * rows :].astype(BF)
    stores = [
        pltpu.make_async_copy(result, target, sem_out.at[i])
        for i, (result, target) in enumerate(zip(results, targets))
    ]
    for store in stores:
        store.start()
    for store in stores:
        store.wait()


def finish_body(own, from_behind, from_ahead, d_keys, d_values):
    for which, out in enumerate((d_keys, d_values)):
        out[...] = (
            own[which] + from_behind[which].astype(F32) + from_ahead[which].astype(F32)
        ).astype(BF)


def vmem():
    return pl.BlockSpec(memory_space=pltpu.VMEM)


def smem():
    return pl.BlockSpec(memory_space=pltpu.SMEM)


def hbm():
    return pl.BlockSpec(memory_space=pltpu.HBM)


def in_hbm(value):
    return pltpu.with_memory_space_constraint(value, pltpu.HBM)


PARAMS = pltpu.CompilerParams(vmem_limit_bytes=20 << 20)


def call(body, outs, specs, scratch=()):
    return pl.pallas_call(
        body,
        out_shape=tuple(jax.ShapeDtypeStruct(shape, dtype) for shape, dtype in outs),
        in_specs=specs,
        out_specs=tuple(vmem() for _ in outs),
        scratch_shapes=scratch,
        compiler_params=PARAMS,
    )


def shift(value, by):
    length = lax.axis_size(REGION)
    return lax.ppermute(value, REGION, [(i, (i + by) % length) for i in range(length)])


def spread_out(value, ways):
    return jnp.broadcast_to(value[None], (ways,) + value.shape)


def local(queries, keys, values, attn_out, d_out, w_out, adjacency, counts):
    queries, keys, values, attn_out, d_out = (
        a[0] for a in (queries, keys, values, attn_out, d_out)
    )
    rows, hw = queries.shape
    width = d_out.shape[1]
    samples = lax.axis_size(DP)
    cores = lax.axis_size("core")
    chips = lax.axis_size("y")
    down = lax.axis_size("x")
    across = lax.axis_size("z_hi")
    part = width // down
    half = HD // cores

    core = lax.axis_index("core").reshape(1)
    w_half, spread, grads, halo = pl.pallas_call(
        prepare_body,
        out_shape=(
            pltpu.HBM((half, width), BF),
            pltpu.HBM((samples, 2 * rows, part), BF),
            pltpu.HBM((rows, width), BF),
            pltpu.HBM((2 * rows + 8, hw), BF),
        ),
        in_specs=[smem()] * 2 + [hbm()] * 5,
        out_specs=(hbm(),) * 4,
        scratch_shapes=[
            pltpu.VMEM((half, width), BF),
            pltpu.VMEM((rows, width), BF),
            pltpu.VMEM((rows, hw), BF),
            pltpu.VMEM((8, hw), BF),
            pltpu.VMEM((2 * rows, hw), BF),
            pltpu.SemaphoreType.DMA((5,)),
            pltpu.SemaphoreType.DMA((samples,)),
            pltpu.SemaphoreType.DMA((samples,)),
            pltpu.SemaphoreType.DMA((4,)),
        ],
        compiler_params=PARAMS,
    )(counts, core, *(in_hbm(a) for a in (d_out, attn_out, keys, values, w_out)))
    w_all = lax.all_gather(w_half, DP + ("core",), axis=0, tiled=True)

    gathered = lax.all_to_all(spread, DP, 0, 0)

    group = 2
    share = -(-(half * part // LANES) // (8 * chips)) * 8
    pieces = (cores, chips, down, share, LANES)
    weight = pl.pallas_call(
        weight_body,
        out_shape=jax.ShapeDtypeStruct(pieces, BF),
        grid=(samples // group,),
        in_specs=[pl.BlockSpec((group, 2 * rows, part), lambda i: (i, 0, 0))],
        out_specs=pl.BlockSpec(pieces, lambda i: (0, 0, 0, 0, 0)),
        scratch_shapes=[pltpu.VMEM((part, part), F32)],
        compiler_params=PARAMS,
    )(gathered)

    pair = lax.all_to_all(weight, "core", 0, 0)
    terms = jnp.sum(pair.astype(F32), axis=0).astype(BF)
    terms, halo = lax.optimization_barrier((terms, halo))
    behind = shift(halo, 1)
    ahead = shift(halo, -1)
    terms = lax.all_to_all(terms, "y", 0, 0)
    terms = jnp.sum(terms.astype(F32), axis=0).astype(BF)
    terms = jnp.broadcast_to(terms[:, None], (down, across, share, LANES))
    terms = terms.reshape(down * across, share, LANES)
    terms, grads = lax.optimization_barrier((terms, grads))
    operands = (
        w_all.reshape(HEADS, HD, width), queries, keys, behind, ahead, grads, attn_out, values,
    )
    pairs = (2, rows, hw)
    results = (((rows, hw), BF), (pairs, F32), (pairs, BF), (pairs, BF))
    d_queries, own, to_behind, to_ahead = pl.pallas_call(
        attention_body,
        out_shape=tuple(pltpu.HBM(shape, dtype) for shape, dtype in results),
        in_specs=[smem()] * 2 + [hbm()] * len(operands),
        out_specs=(hbm(),) * len(results),
        scratch_shapes=[pltpu.VMEM(a.shape, a.dtype) for a in operands]
        + [pltpu.VMEM(shape, dtype) for shape, dtype in results]
        + [
            pltpu.SemaphoreType.DMA((HEADS,)),
            pltpu.SemaphoreType.DMA((len(operands) - 1,)),
            pltpu.SemaphoreType.DMA((len(results),)),
        ],
        compiler_params=PARAMS,
    )(counts, adjacency[0], *(in_hbm(a) for a in operands))
    terms = lax.all_to_all(terms, ("x", "z_hi"), 0, 0).reshape(down, across, share, LANES)
    terms, own = lax.optimization_barrier((terms, own))
    total = jnp.sum(terms.astype(F32), axis=1).astype(BF)
    total = lax.all_to_all(spread_out(total, chips), "y", 0, 0)
    both = lax.all_to_all(spread_out(total, cores), "core", 0, 0)
    (d_weight,) = call(assemble_body, [((HD, width), BF)], [vmem()])(both)

    d_weight, own = lax.optimization_barrier((d_weight, own))
    d_keys, d_values = call(
        finish_body, [((rows, hw), BF), ((rows, hw), BF)], [vmem()] * 3
    )(own, shift(to_ahead, 1), shift(to_behind, -1))
    return d_queries[None], d_keys[None], d_values[None], d_weight


def solution(mesh):
    parts = Mesh(mesh.devices.reshape(2, 4, 8, 4, 2), DP + REGION)
    rows = P(DP, REGION, None)
    return jax.shard_map(
        local,
        mesh=parts,
        in_specs=(rows, rows, rows, rows, rows, P(DP, None), P(REGION, None, None), P(REGION)),
        out_specs=(rows, rows, rows, P(DP, None)),
        check_vma=False,
    )
```

```python
import math

import jax
import jax.numpy as jnp
from jax import lax
from jax.experimental import pallas as pl
from jax.experimental.pallas import tpu as pltpu
from jax.sharding import Mesh
from jax.sharding import PartitionSpec as P

HEADS = 8
HD = 160
BLK = 4
DP = ("z_lo", "x")
REGION = ("y", "z_hi", "core")
BF = jnp.bfloat16
F32 = jnp.float32
LANES = 128
SCALE = 1.0 / math.sqrt(HD)


def nn(a, b):
    return lax.dot_general(a, b, (((1,), (0,)), ((), ())), preferred_element_type=F32)


def nt(a, b):
    return lax.dot_general(a, b, (((1,), (1,)), ((), ())), preferred_element_type=F32)


def tn(a, b):
    return lax.dot_general(a, b, (((0,), (0,)), ((), ())), preferred_element_type=F32)


def prepare_body(
    counts, core, d_out, attn_out, keys, values, w_out, w_half, spread, grads, halo,
    w_in, grads_in, attn_in, tail, halo_in, sem_in, sem_attn, sem_out, sem_halo,
):
    rows, width = d_out.shape
    samples, _, part = spread.shape
    down = width // part
    half_rows = w_half.shape[0]
    first_row = pl.multiple_of(core[0] * half_rows, half_rows)
    w_load = pltpu.make_async_copy(w_out.at[pl.ds(first_row, half_rows)], w_in, sem_in.at[4])
    w_load.start()
    loads = [
        pltpu.make_async_copy(d_out, grads_in, sem_in.at[0]),
        pltpu.make_async_copy(attn_out, attn_in, sem_in.at[1]),
        pltpu.make_async_copy(keys, halo_in.at[pl.ds(0, rows)], sem_in.at[2]),
        pltpu.make_async_copy(values, halo_in.at[pl.ds(rows, rows)], sem_in.at[3]),
    ]
    for load in loads:
        load.start()
    tail[...] = jnp.full(tail.shape, counts[0].astype(F32), F32).astype(BF)
    stores = [pltpu.make_async_copy(tail, halo.at[pl.ds(2 * rows, 8)], sem_halo.at[1])]
    live = lax.broadcasted_iota(jnp.int32, (rows, 1), 0) // (rows // BLK) < counts[0]
    w_load.wait()
    stores.append(pltpu.make_async_copy(w_in, w_half, sem_halo.at[3]))
    loads[0].wait()
    grads_in[...] = jnp.where(live, grads_in[...], jnp.zeros((), BF))
    for s in range(samples):
        quarter = pl.ds(s % down * part, part)
        stores.append(
            pltpu.make_async_copy(
                grads_in.at[:, quarter], spread.at[s, pl.ds(rows, rows)], sem_out.at[s]
            )
        )
    stores.append(pltpu.make_async_copy(grads_in, grads, sem_halo.at[2]))
    for store in stores:
        store.start()
    loads[1].wait()
    for s in range(samples):
        half = pl.ds(s // down * part, part)
        stores.append(
            pltpu.make_async_copy(
                attn_in.at[:, half], spread.at[s, pl.ds(0, rows)], sem_attn.at[s]
            )
        )
        stores[-1].start()
    loads[2].wait()
    loads[3].wait()
    stores.append(
        pltpu.make_async_copy(halo_in, halo.at[pl.ds(0, 2 * rows)], sem_halo.at[0])
    )
    stores[-1].start()
    for store in stores:
        store.wait()


def allowed_pairs(counts, adjacency, behind, ahead, rows):
    block = rows // BLK
    width = 3 * rows
    key_block = lax.broadcasted_iota(jnp.int32, (1, width), 1) // block
    count = jnp.concatenate(
        [
            behind[2 * rows : 2 * rows + 1, :rows].astype(F32),
            jnp.full((1, rows), counts[0].astype(F32), F32),
            ahead[2 * rows : 2 * rows + 1, :rows].astype(F32),
        ],
        1,
    )
    live = (key_block % BLK).astype(F32) < count
    bias = []
    for a in range(BLK):
        seen = jnp.zeros((1, width), jnp.int32)
        for j in range(3 * BLK):
            seen = jnp.where(key_block == j, adjacency[a, j], seen)
        ok = jnp.logical_or(jnp.logical_and(seen == 1, live), key_block == BLK + a)
        bias.append(jnp.broadcast_to(jnp.where(ok, 1.0, 0.0), (block, width)))
    return jnp.concatenate(bias, 0) > 0.5


def weight_body(gathered, weight, acc):
    step = pl.program_id(0)
    samples, both, part = gathered.shape
    cores, chips, heads, share, _ = weight.shape
    rows = both // 2
    left = gathered[:, :rows, :].reshape(samples * rows, part)
    right = gathered[:, rows:, :].reshape(samples * rows, part)
    term = tn(left, right)

    @pl.when(step == 0)
    def _():
        acc[...] = term

    @pl.when(step > 0)
    def _():
        acc[...] += term

    @pl.when(step == pl.num_programs(0) - 1)
    def _():
        half = HD // cores
        tiles = part // LANES
        for c in range(cores):
            for h in range(heads):
                first = h * HD + c * half
                pieces = [
                    acc[first : first + half, j * LANES : (j + 1) * LANES] for j in range(tiles)
                ]
                pieces.append(jnp.zeros((chips * share - tiles * half, LANES), F32))
                flat = jnp.concatenate(pieces, 0).reshape(chips, share, LANES)
                for m in range(chips):
                    weight[c, m, h] = flat[m].astype(BF)


def assemble_body(both, d_weight):
    cores, chips, quarters, _, _ = both.shape
    half = HD // cores
    part = d_weight.shape[1] // quarters
    for c in range(cores):
        for q in range(quarters):
            flat = jnp.concatenate([both[c, m, q].astype(F32) for m in range(chips)], 0)
            for j in range(part // LANES):
                first = q * part + j * LANES
                d_weight[c * half : (c + 1) * half, first : first + LANES] = flat[
                    j * half : (j + 1) * half
                ].astype(BF)


def project_body(w_all, grads, d_attn, w_in, grads_in, sem_w, sem):
    load = pltpu.make_async_copy(grads, grads_in, sem.at[0])
    w_loads = [pltpu.make_async_copy(w_all.at[h], w_in.at[h], sem_w.at[h]) for h in range(HEADS)]
    load.start()
    for w_load in w_loads:
        w_load.start()
    load.wait()
    for h in range(HEADS):
        w_loads[h].wait()
        d_attn[:, h * HD : (h + 1) * HD] = nt(grads_in[...], w_in[h]).astype(BF)


def attention_body(counts, adjacency, d_attn, behind, ahead, *refs):
    sources, rest = refs[:4], refs[4:]
    targets, rest = rest[:4], rest[4:]
    arrays, rest = rest[:4], rest[4:]
    results, (sem_in, sem_out) = rest[:4], rest[4:]
    queries, keys, attn_out, values = arrays
    d_queries, own, to_behind, to_ahead = results
    rows = queries.shape[0]
    loads = [
        pltpu.make_async_copy(source, array, sem_in.at[i])
        for i, (source, array) in enumerate(zip(sources, arrays))
    ]
    for load in loads:
        load.start()
    for load in loads:
        load.wait()
    allowed = allowed_pairs(counts, adjacency, behind, ahead, rows)
    for h in range(HEADS):
        cols = slice(h * HD, (h + 1) * HD)
        key_win = jnp.concatenate([behind[0:rows, cols], keys[:, cols], ahead[0:rows, cols]], 0)
        query = queries[:, cols]
        scores = jnp.where(allowed, nt(query, key_win) * SCALE, -1e30)
        terms = jnp.exp(scores - jnp.max(scores, axis=1, keepdims=True))
        terms = jnp.where(allowed, terms, 0.0)
        prob = terms / jnp.sum(terms, axis=1, keepdims=True)
        grad = d_attn[:, cols]
        delta = jnp.sum(
            grad.astype(F32) * attn_out[:, cols].astype(F32), axis=1, keepdims=True
        )
        value_win = jnp.concatenate(
            [behind[rows : 2 * rows, cols], values[:, cols], ahead[rows : 2 * rows, cols]], 0
        )
        dprobs = nt(grad, value_win)
        dscores = (prob * (dprobs - delta) * SCALE).astype(BF)
        d_queries[:, cols] = nn(dscores, key_win).astype(BF)
        for which, (left, right) in enumerate(((dscores, query), (prob.astype(BF), grad))):
            win = tn(left, right)
            to_behind[which, :, cols] = win[:rows].astype(BF)
            own[which, :, cols] = win[rows : 2 * rows]
            to_ahead[which, :, cols] = win[2 * rows :].astype(BF)
    stores = [
        pltpu.make_async_copy(result, target, sem_out.at[i])
        for i, (result, target) in enumerate(zip(results, targets))
    ]
    for store in stores:
        store.start()
    for store in stores:
        store.wait()


def finish_body(own, from_behind, from_ahead, d_keys, d_values):
    for which, out in enumerate((d_keys, d_values)):
        out[...] = (
            own[which] + from_behind[which].astype(F32) + from_ahead[which].astype(F32)
        ).astype(BF)


def vmem():
    return pl.BlockSpec(memory_space=pltpu.VMEM)


def smem():
    return pl.BlockSpec(memory_space=pltpu.SMEM)


def hbm():
    return pl.BlockSpec(memory_space=pltpu.HBM)


def in_hbm(value):
    return pltpu.with_memory_space_constraint(value, pltpu.HBM)


PARAMS = pltpu.CompilerParams(vmem_limit_bytes=20 << 20)


def call(body, outs, specs, scratch=()):
    return pl.pallas_call(
        body,
        out_shape=tuple(jax.ShapeDtypeStruct(shape, dtype) for shape, dtype in outs),
        in_specs=specs,
        out_specs=tuple(vmem() for _ in outs),
        scratch_shapes=scratch,
        compiler_params=PARAMS,
    )


def shift(value, by):
    length = lax.axis_size(REGION)
    return lax.ppermute(value, REGION, [(i, (i + by) % length) for i in range(length)])


def spread_out(value, ways):
    return jnp.broadcast_to(value[None], (ways,) + value.shape)


def local(queries, keys, values, attn_out, d_out, w_out, adjacency, counts):
    queries, keys, values, attn_out, d_out = (
        a[0] for a in (queries, keys, values, attn_out, d_out)
    )
    rows, hw = queries.shape
    width = d_out.shape[1]
    samples = lax.axis_size(DP)
    cores = lax.axis_size("core")
    chips = lax.axis_size("y")
    down = lax.axis_size("x")
    across = lax.axis_size("z_hi")
    part = width // down
    half = HD // cores

    core = lax.axis_index("core").reshape(1)
    w_half, spread, grads, halo = pl.pallas_call(
        prepare_body,
        out_shape=(
            pltpu.HBM((half, width), BF),
            pltpu.HBM((samples, 2 * rows, part), BF),
            pltpu.HBM((rows, width), BF),
            pltpu.HBM((2 * rows + 8, hw), BF),
        ),
        in_specs=[smem()] * 2 + [hbm()] * 5,
        out_specs=(hbm(),) * 4,
        scratch_shapes=[
            pltpu.VMEM((half, width), BF),
            pltpu.VMEM((rows, width), BF),
            pltpu.VMEM((rows, hw), BF),
            pltpu.VMEM((8, hw), BF),
            pltpu.VMEM((2 * rows, hw), BF),
            pltpu.SemaphoreType.DMA((5,)),
            pltpu.SemaphoreType.DMA((samples,)),
            pltpu.SemaphoreType.DMA((samples,)),
            pltpu.SemaphoreType.DMA((4,)),
        ],
        compiler_params=PARAMS,
    )(counts, core, *(in_hbm(a) for a in (d_out, attn_out, keys, values, w_out)))
    w_all = lax.all_gather(w_half, DP + ("core",), axis=0, tiled=True)

    gathered = lax.all_to_all(spread, DP, 0, 0)

    group = 2
    share = -(-(half * part // LANES) // (8 * chips)) * 8
    pieces = (cores, chips, down, share, LANES)
    weight = pl.pallas_call(
        weight_body,
        out_shape=jax.ShapeDtypeStruct(pieces, BF),
        grid=(samples // group,),
        in_specs=[pl.BlockSpec((group, 2 * rows, part), lambda i: (i, 0, 0))],
        out_specs=pl.BlockSpec(pieces, lambda i: (0, 0, 0, 0, 0)),
        scratch_shapes=[pltpu.VMEM((part, part), F32)],
        compiler_params=PARAMS,
    )(gathered)

    pair = lax.all_to_all(weight, "core", 0, 0)
    terms = jnp.sum(pair.astype(F32), axis=0).astype(BF)
    terms, halo = lax.optimization_barrier((terms, halo))
    behind = shift(halo, 1)
    ahead = shift(halo, -1)
    terms = lax.all_to_all(terms, "y", 0, 0)
    terms = jnp.sum(terms.astype(F32), axis=0).astype(BF)
    terms = jnp.broadcast_to(terms[:, None], (down, across, share, LANES))
    terms = terms.reshape(down * across, share, LANES)
    terms, grads = lax.optimization_barrier((terms, grads))
    (d_attn,) = call(
        project_body,
        [((rows, hw), BF)],
        [hbm(), hbm()],
        [
            pltpu.VMEM((HEADS, HD, width), BF),
            pltpu.VMEM((rows, width), BF),
            pltpu.SemaphoreType.DMA((HEADS,)),
            pltpu.SemaphoreType.DMA((1,)),
        ],
    )(in_hbm(w_all.reshape(HEADS, HD, width)), in_hbm(grads))
    operands = (queries, keys, attn_out, values)
    pairs = (2, rows, hw)
    results = (((rows, hw), BF), (pairs, F32), (pairs, BF), (pairs, BF))
    d_queries, own, to_behind, to_ahead = pl.pallas_call(
        attention_body,
        out_shape=tuple(pltpu.HBM(shape, dtype) for shape, dtype in results),
        in_specs=[smem()] * 2 + [vmem()] * 3 + [hbm()] * len(operands),
        out_specs=(hbm(),) * len(results),
        scratch_shapes=[pltpu.VMEM(a.shape, a.dtype) for a in operands]
        + [pltpu.VMEM(shape, dtype) for shape, dtype in results]
        + [
            pltpu.SemaphoreType.DMA((len(operands),)),
            pltpu.SemaphoreType.DMA((len(results),)),
        ],
        compiler_params=PARAMS,
    )(counts, adjacency[0], d_attn, behind, ahead, *(in_hbm(a) for a in operands))
    terms = lax.all_to_all(terms, ("x", "z_hi"), 0, 0).reshape(down, across, share, LANES)
    terms, own = lax.optimization_barrier((terms, own))
    total = jnp.sum(terms.astype(F32), axis=1).astype(BF)
    total = lax.all_to_all(spread_out(total, chips), "y", 0, 0)
    both = lax.all_to_all(spread_out(total, cores), "core", 0, 0)
    (d_weight,) = call(assemble_body, [((HD, width), BF)], [vmem()])(both)

    d_weight, own = lax.optimization_barrier((d_weight, own))
    d_keys, d_values = call(
        finish_body, [((rows, hw), BF), ((rows, hw), BF)], [vmem()] * 3
    )(own, shift(to_ahead, 1), shift(to_behind, -1))
    return d_queries[None], d_keys[None], d_values[None], d_weight


def solution(mesh):
    parts = Mesh(mesh.devices.reshape(2, 4, 8, 4, 2), DP + REGION)
    rows = P(DP, REGION, None)
    return jax.shard_map(
        local,
        mesh=parts,
        in_specs=(rows, rows, rows, rows, rows, P(DP, None), P(REGION, None, None), P(REGION)),
        out_specs=(rows, rows, rows, P(DP, None)),
        check_vma=False,
    )
```

```python
import math

import jax
import jax.numpy as jnp
from jax import lax
from jax.experimental import pallas as pl
from jax.experimental.pallas import tpu as pltpu
from jax.sharding import Mesh
from jax.sharding import PartitionSpec as P

HEADS = 8
HD = 160
BLK = 4
DP = ("z_lo", "x")
REGION = ("y", "z_hi", "core")
BF = jnp.bfloat16
F32 = jnp.float32
LANES = 128
SCALE = 1.0 / math.sqrt(HD)


def nn(a, b):
    return lax.dot_general(a, b, (((1,), (0,)), ((), ())), preferred_element_type=F32)


def nt(a, b):
    return lax.dot_general(a, b, (((1,), (1,)), ((), ())), preferred_element_type=F32)


def tn(a, b):
    return lax.dot_general(a, b, (((0,), (0,)), ((), ())), preferred_element_type=F32)


def prepare_body(
    counts, core, d_out, attn_out, keys, values, w_out, w_half, spread, grads, halo,
    w_in, grads_in, attn_in, tail, halo_in, sem_in, sem_attn, sem_out, sem_halo,
):
    rows, width = d_out.shape
    samples, _, part = spread.shape
    down = width // part
    half_rows = w_half.shape[0]
    first_row = pl.multiple_of(core[0] * half_rows, half_rows)
    w_load = pltpu.make_async_copy(w_out.at[pl.ds(first_row, half_rows)], w_in, sem_in.at[4])
    w_load.start()
    loads = [
        pltpu.make_async_copy(d_out, grads_in, sem_in.at[0]),
        pltpu.make_async_copy(attn_out, attn_in, sem_in.at[1]),
        pltpu.make_async_copy(keys, halo_in.at[pl.ds(0, rows)], sem_in.at[2]),
        pltpu.make_async_copy(values, halo_in.at[pl.ds(rows, rows)], sem_in.at[3]),
    ]
    for load in loads:
        load.start()
    tail[...] = jnp.full(tail.shape, counts[0].astype(F32), F32).astype(BF)
    stores = [pltpu.make_async_copy(tail, halo.at[pl.ds(2 * rows, 8)], sem_halo.at[1])]
    live = lax.broadcasted_iota(jnp.int32, (rows, 1), 0) // (rows // BLK) < counts[0]
    w_load.wait()
    stores.append(pltpu.make_async_copy(w_in, w_half, sem_halo.at[3]))
    loads[0].wait()
    grads_in[...] = jnp.where(live, grads_in[...], jnp.zeros((), BF))
    for s in range(samples):
        quarter = pl.ds(s % down * part, part)
        stores.append(
            pltpu.make_async_copy(
                grads_in.at[:, quarter], spread.at[s, pl.ds(rows, rows)], sem_out.at[s]
            )
        )
    stores.append(pltpu.make_async_copy(grads_in, grads, sem_halo.at[2]))
    for store in stores:
        store.start()
    loads[1].wait()
    for s in range(samples):
        half = pl.ds(s // down * part, part)
        stores.append(
            pltpu.make_async_copy(
                attn_in.at[:, half], spread.at[s, pl.ds(0, rows)], sem_attn.at[s]
            )
        )
        stores[-1].start()
    loads[2].wait()
    loads[3].wait()
    stores.append(
        pltpu.make_async_copy(halo_in, halo.at[pl.ds(0, 2 * rows)], sem_halo.at[0])
    )
    stores[-1].start()
    for store in stores:
        store.wait()


def allowed_pairs(counts, adjacency, behind, ahead, rows):
    block = rows // BLK
    width = 3 * rows
    key_block = lax.broadcasted_iota(jnp.int32, (1, width), 1) // block
    count = jnp.concatenate(
        [
            behind[2 * rows : 2 * rows + 1, :rows].astype(F32),
            jnp.full((1, rows), counts[0].astype(F32), F32),
            ahead[2 * rows : 2 * rows + 1, :rows].astype(F32),
        ],
        1,
    )
    live = (key_block % BLK).astype(F32) < count
    bias = []
    for a in range(BLK):
        seen = jnp.zeros((1, width), jnp.int32)
        for j in range(3 * BLK):
            seen = jnp.where(key_block == j, adjacency[a, j], seen)
        ok = jnp.logical_or(jnp.logical_and(seen == 1, live), key_block == BLK + a)
        bias.append(jnp.broadcast_to(jnp.where(ok, 1.0, 0.0), (block, width)))
    return jnp.concatenate(bias, 0) > 0.5


def weight_body(gathered, weight, acc):
    step = pl.program_id(0)
    samples, both, part = gathered.shape
    cores, chips, heads, share, _ = weight.shape
    rows = both // 2
    left = gathered[:, :rows, :].reshape(samples * rows, part)
    right = gathered[:, rows:, :].reshape(samples * rows, part)
    term = tn(left, right)

    @pl.when(step == 0)
    def _():
        acc[...] = term

    @pl.when(step > 0)
    def _():
        acc[...] += term

    @pl.when(step == pl.num_programs(0) - 1)
    def _():
        half = HD // cores
        tiles = part // LANES
        for c in range(cores):
            for h in range(heads):
                first = h * HD + c * half
                pieces = [
                    acc[first : first + half, j * LANES : (j + 1) * LANES] for j in range(tiles)
                ]
                pieces.append(jnp.zeros((chips * share - tiles * half, LANES), F32))
                flat = jnp.concatenate(pieces, 0).reshape(chips, share, LANES)
                for m in range(chips):
                    weight[c, m, h] = flat[m].astype(BF)


def assemble_body(both, d_weight):
    cores, chips, quarters, _, _ = both.shape
    half = HD // cores
    part = d_weight.shape[1] // quarters
    for c in range(cores):
        for q in range(quarters):
            flat = jnp.concatenate([both[c, m, q].astype(F32) for m in range(chips)], 0)
            for j in range(part // LANES):
                first = q * part + j * LANES
                d_weight[c * half : (c + 1) * half, first : first + LANES] = flat[
                    j * half : (j + 1) * half
                ].astype(BF)


def project_body(w_all, grads, d_attn, w_in, grads_in, sem_w, sem):
    load = pltpu.make_async_copy(grads, grads_in, sem.at[0])
    w_loads = [pltpu.make_async_copy(w_all.at[h], w_in.at[h], sem_w.at[h]) for h in range(HEADS)]
    load.start()
    for w_load in w_loads:
        w_load.start()
    load.wait()
    for h in range(HEADS):
        w_loads[h].wait()
        d_attn[:, h * HD : (h + 1) * HD] = nt(grads_in[...], w_in[h]).astype(BF)


def attention_body(counts, adjacency, d_attn, behind, ahead, *refs):
    sources, rest = refs[:4], refs[4:]
    targets, rest = rest[:4], rest[4:]
    arrays, rest = rest[:4], rest[4:]
    results, (sem_in, sem_out) = rest[:4], rest[4:]
    queries, keys, attn_out, values = arrays
    d_queries, own, to_behind, to_ahead = results
    rows = queries.shape[0]
    loads = [
        pltpu.make_async_copy(source, array, sem_in.at[i])
        for i, (source, array) in enumerate(zip(sources, arrays))
    ]
    for load in loads:
        load.start()
    for load in loads:
        load.wait()
    allowed = allowed_pairs(counts, adjacency, behind, ahead, rows)
    for h in range(HEADS):
        cols = slice(h * HD, (h + 1) * HD)
        key_win = jnp.concatenate([behind[0:rows, cols], keys[:, cols], ahead[0:rows, cols]], 0)
        query = queries[:, cols]
        scores = jnp.where(allowed, nt(query, key_win) * SCALE, -1e30)
        terms = jnp.exp(scores - jnp.max(scores, axis=1, keepdims=True))
        terms = jnp.where(allowed, terms, 0.0)
        prob = terms / jnp.sum(terms, axis=1, keepdims=True)
        grad = d_attn[:, cols]
        delta = jnp.sum(
            grad.astype(F32) * attn_out[:, cols].astype(F32), axis=1, keepdims=True
        )
        value_win = jnp.concatenate(
            [behind[rows : 2 * rows, cols], values[:, cols], ahead[rows : 2 * rows, cols]], 0
        )
        dprobs = nt(grad, value_win)
        dscores = (prob * (dprobs - delta) * SCALE).astype(BF)
        d_queries[:, cols] = nn(dscores, key_win).astype(BF)
        for which, (left, right) in enumerate(((dscores, query), (prob.astype(BF), grad))):
            win = tn(left, right)
            to_behind[which, :, cols] = win[:rows].astype(BF)
            own[which, :, cols] = win[rows : 2 * rows]
            to_ahead[which, :, cols] = win[2 * rows :].astype(BF)
    stores = [
        pltpu.make_async_copy(result, target, sem_out.at[i])
        for i, (result, target) in enumerate(zip(results, targets))
    ]
    for store in stores:
        store.start()
    for store in stores:
        store.wait()


def finish_body(own, from_behind, from_ahead, d_keys, d_values):
    for which, out in enumerate((d_keys, d_values)):
        out[...] = (
            own[which] + from_behind[which].astype(F32) + from_ahead[which].astype(F32)
        ).astype(BF)


def vmem():
    return pl.BlockSpec(memory_space=pltpu.VMEM)


def smem():
    return pl.BlockSpec(memory_space=pltpu.SMEM)


def hbm():
    return pl.BlockSpec(memory_space=pltpu.HBM)


def in_hbm(value):
    return pltpu.with_memory_space_constraint(value, pltpu.HBM)


PARAMS = pltpu.CompilerParams(vmem_limit_bytes=20 << 20)


def call(body, outs, specs, scratch=()):
    return pl.pallas_call(
        body,
        out_shape=tuple(jax.ShapeDtypeStruct(shape, dtype) for shape, dtype in outs),
        in_specs=specs,
        out_specs=tuple(vmem() for _ in outs),
        scratch_shapes=scratch,
        compiler_params=PARAMS,
    )


def shift(value, by):
    length = lax.axis_size(REGION)
    return lax.ppermute(value, REGION, [(i, (i + by) % length) for i in range(length)])


def spread_out(value, ways):
    return jnp.broadcast_to(value[None], (ways,) + value.shape)


def local(queries, keys, values, attn_out, d_out, w_out, adjacency, counts):
    queries, keys, values, attn_out, d_out = (
        a[0] for a in (queries, keys, values, attn_out, d_out)
    )
    rows, hw = queries.shape
    width = d_out.shape[1]
    samples = lax.axis_size(DP)
    cores = lax.axis_size("core")
    chips = lax.axis_size("y")
    down = lax.axis_size("x")
    across = lax.axis_size("z_hi")
    part = width // down
    half = HD // cores

    core = lax.axis_index("core").reshape(1)
    w_half, spread, grads, halo = pl.pallas_call(
        prepare_body,
        out_shape=(
            pltpu.HBM((half, width), BF),
            pltpu.HBM((samples, 2 * rows, part), BF),
            pltpu.HBM((rows, width), BF),
            pltpu.HBM((2 * rows + 8, hw), BF),
        ),
        in_specs=[smem()] * 2 + [hbm()] * 5,
        out_specs=(hbm(),) * 4,
        scratch_shapes=[
            pltpu.VMEM((half, width), BF),
            pltpu.VMEM((rows, width), BF),
            pltpu.VMEM((rows, hw), BF),
            pltpu.VMEM((8, hw), BF),
            pltpu.VMEM((2 * rows, hw), BF),
            pltpu.SemaphoreType.DMA((5,)),
            pltpu.SemaphoreType.DMA((samples,)),
            pltpu.SemaphoreType.DMA((samples,)),
            pltpu.SemaphoreType.DMA((4,)),
        ],
        compiler_params=PARAMS,
    )(counts, core, *(in_hbm(a) for a in (d_out, attn_out, keys, values, w_out)))
    w_all = lax.all_gather(w_half, DP + ("core",), axis=0, tiled=True)

    gathered = lax.all_to_all(spread, DP, 0, 0)

    group = 2
    share = -(-(half * part // LANES) // (8 * chips)) * 8
    pieces = (cores, chips, down, share, LANES)
    weight = pl.pallas_call(
        weight_body,
        out_shape=jax.ShapeDtypeStruct(pieces, BF),
        grid=(samples // group,),
        in_specs=[pl.BlockSpec((group, 2 * rows, part), lambda i: (i, 0, 0))],
        out_specs=pl.BlockSpec(pieces, lambda i: (0, 0, 0, 0, 0)),
        scratch_shapes=[pltpu.VMEM((part, part), F32)],
        compiler_params=PARAMS,
    )(gathered)

    pair = lax.all_to_all(weight, "core", 0, 0)
    terms = jnp.sum(pair.astype(F32), axis=0).astype(BF)
    terms, halo, grads = lax.optimization_barrier((terms, halo, grads))
    (d_attn,) = call(
        project_body,
        [((rows, hw), BF)],
        [hbm(), hbm()],
        [
            pltpu.VMEM((HEADS, HD, width), BF),
            pltpu.VMEM((rows, width), BF),
            pltpu.SemaphoreType.DMA((HEADS,)),
            pltpu.SemaphoreType.DMA((1,)),
        ],
    )(in_hbm(w_all.reshape(HEADS, HD, width)), in_hbm(grads))
    behind = shift(halo, 1)
    ahead = shift(halo, -1)
    terms = lax.all_to_all(terms, "y", 0, 0)
    terms, d_attn = lax.optimization_barrier((terms, d_attn))
    terms = jnp.sum(terms.astype(F32), axis=0).astype(BF)
    terms = jnp.broadcast_to(terms[:, None], (down, across, share, LANES))
    terms = terms.reshape(down * across, share, LANES)
    terms, d_attn = lax.optimization_barrier((terms, d_attn))
    operands = (queries, keys, attn_out, values)
    pairs = (2, rows, hw)
    results = (((rows, hw), BF), (pairs, F32), (pairs, BF), (pairs, BF))
    d_queries, own, to_behind, to_ahead = pl.pallas_call(
        attention_body,
        out_shape=tuple(pltpu.HBM(shape, dtype) for shape, dtype in results),
        in_specs=[smem()] * 2 + [vmem()] * 3 + [hbm()] * len(operands),
        out_specs=(hbm(),) * len(results),
        scratch_shapes=[pltpu.VMEM(a.shape, a.dtype) for a in operands]
        + [pltpu.VMEM(shape, dtype) for shape, dtype in results]
        + [
            pltpu.SemaphoreType.DMA((len(operands),)),
            pltpu.SemaphoreType.DMA((len(results),)),
        ],
        compiler_params=PARAMS,
    )(counts, adjacency[0], d_attn, behind, ahead, *(in_hbm(a) for a in operands))
    terms = lax.all_to_all(terms, ("x", "z_hi"), 0, 0).reshape(down, across, share, LANES)
    terms, own = lax.optimization_barrier((terms, own))
    total = jnp.sum(terms.astype(F32), axis=1).astype(BF)
    total = lax.all_to_all(spread_out(total, chips), "y", 0, 0)
    both = lax.all_to_all(spread_out(total, cores), "core", 0, 0)
    (d_weight,) = call(assemble_body, [((HD, width), BF)], [vmem()])(both)

    d_weight, own = lax.optimization_barrier((d_weight, own))
    d_keys, d_values = call(
        finish_body, [((rows, hw), BF), ((rows, hw), BF)], [vmem()] * 3
    )(own, shift(to_ahead, 1), shift(to_behind, -1))
    return d_queries[None], d_keys[None], d_values[None], d_weight


def solution(mesh):
    parts = Mesh(mesh.devices.reshape(2, 4, 8, 4, 2), DP + REGION)
    rows = P(DP, REGION, None)
    return jax.shard_map(
        local,
        mesh=parts,
        in_specs=(rows, rows, rows, rows, rows, P(DP, None), P(REGION, None, None), P(REGION)),
        out_specs=(rows, rows, rows, P(DP, None)),
        check_vma=False,
    )
```

```python
import math

import jax
import jax.numpy as jnp
from jax import lax
from jax.experimental import pallas as pl
from jax.experimental.pallas import tpu as pltpu
from jax.sharding import Mesh
from jax.sharding import PartitionSpec as P

HEADS = 8
HD = 160
BLK = 4
DP = ("z_lo", "x")
REGION = ("y", "z_hi", "core")
BF = jnp.bfloat16
F32 = jnp.float32
LANES = 128
SCALE = 1.0 / math.sqrt(HD)


def nn(a, b):
    return lax.dot_general(a, b, (((1,), (0,)), ((), ())), preferred_element_type=F32)


def nt(a, b):
    return lax.dot_general(a, b, (((1,), (1,)), ((), ())), preferred_element_type=F32)


def tn(a, b):
    return lax.dot_general(a, b, (((0,), (0,)), ((), ())), preferred_element_type=F32)


def prepare_body(
    counts, core, d_out, attn_out, keys, values, w_out, w_half, spread, grads, halo,
    w_in, grads_in, attn_in, tail, halo_in, sem_in, sem_attn, sem_out, sem_halo,
):
    rows, width = d_out.shape
    samples, _, part = spread.shape
    down = width // part
    half_rows = w_half.shape[0]
    first_row = pl.multiple_of(core[0] * half_rows, half_rows)
    w_load = pltpu.make_async_copy(w_out.at[pl.ds(first_row, half_rows)], w_in, sem_in.at[4])
    w_load.start()
    loads = [
        pltpu.make_async_copy(d_out, grads_in, sem_in.at[0]),
        pltpu.make_async_copy(attn_out, attn_in, sem_in.at[1]),
        pltpu.make_async_copy(keys, halo_in.at[pl.ds(0, rows)], sem_in.at[2]),
        pltpu.make_async_copy(values, halo_in.at[pl.ds(rows, rows)], sem_in.at[3]),
    ]
    for load in loads:
        load.start()
    tail[...] = jnp.full(tail.shape, counts[0].astype(F32), F32).astype(BF)
    stores = [pltpu.make_async_copy(tail, halo.at[pl.ds(2 * rows, 8)], sem_halo.at[1])]
    live = lax.broadcasted_iota(jnp.int32, (rows, 1), 0) // (rows // BLK) < counts[0]
    w_load.wait()
    stores.append(pltpu.make_async_copy(w_in, w_half, sem_halo.at[3]))
    loads[0].wait()
    grads_in[...] = jnp.where(live, grads_in[...], jnp.zeros((), BF))
    for s in range(samples):
        quarter = pl.ds(s % down * part, part)
        stores.append(
            pltpu.make_async_copy(
                grads_in.at[:, quarter], spread.at[s, pl.ds(rows, rows)], sem_out.at[s]
            )
        )
    stores.append(pltpu.make_async_copy(grads_in, grads, sem_halo.at[2]))
    for store in stores:
        store.start()
    loads[1].wait()
    for s in range(samples):
        half = pl.ds(s // down * part, part)
        stores.append(
            pltpu.make_async_copy(
                attn_in.at[:, half], spread.at[s, pl.ds(0, rows)], sem_attn.at[s]
            )
        )
        stores[-1].start()
    loads[2].wait()
    loads[3].wait()
    stores.append(
        pltpu.make_async_copy(halo_in, halo.at[pl.ds(0, 2 * rows)], sem_halo.at[0])
    )
    stores[-1].start()
    for store in stores:
        store.wait()


def allowed_pairs(counts, adjacency, behind, ahead, rows):
    block = rows // BLK
    width = 3 * rows
    key_block = lax.broadcasted_iota(jnp.int32, (1, width), 1) // block
    count = jnp.concatenate(
        [
            behind[2 * rows : 2 * rows + 1, :rows].astype(F32),
            jnp.full((1, rows), counts[0].astype(F32), F32),
            ahead[2 * rows : 2 * rows + 1, :rows].astype(F32),
        ],
        1,
    )
    live = (key_block % BLK).astype(F32) < count
    bias = []
    for a in range(BLK):
        seen = jnp.zeros((1, width), jnp.int32)
        for j in range(3 * BLK):
            seen = jnp.where(key_block == j, adjacency[a, j], seen)
        ok = jnp.logical_or(jnp.logical_and(seen == 1, live), key_block == BLK + a)
        bias.append(jnp.broadcast_to(jnp.where(ok, 1.0, 0.0), (block, width)))
    return jnp.concatenate(bias, 0) > 0.5


def weight_body(gathered, weight, acc):
    step = pl.program_id(0)
    samples, both, part = gathered.shape
    cores, chips, heads, share, _ = weight.shape
    rows = both // 2
    left = gathered[:, :rows, :].reshape(samples * rows, part)
    right = gathered[:, rows:, :].reshape(samples * rows, part)
    term = tn(left, right)

    @pl.when(step == 0)
    def _():
        acc[...] = term

    @pl.when(step > 0)
    def _():
        acc[...] += term

    @pl.when(step == pl.num_programs(0) - 1)
    def _():
        half = HD // cores
        tiles = part // LANES
        for c in range(cores):
            for h in range(heads):
                first = h * HD + c * half
                pieces = [
                    acc[first : first + half, j * LANES : (j + 1) * LANES] for j in range(tiles)
                ]
                pieces.append(jnp.zeros((chips * share - tiles * half, LANES), F32))
                flat = jnp.concatenate(pieces, 0).reshape(chips, share, LANES)
                for m in range(chips):
                    weight[c, m, h] = flat[m].astype(BF)


def assemble_body(both, d_weight):
    cores, chips, quarters, _, _ = both.shape
    half = HD // cores
    part = d_weight.shape[1] // quarters
    for c in range(cores):
        for q in range(quarters):
            flat = jnp.concatenate([both[c, m, q].astype(F32) for m in range(chips)], 0)
            for j in range(part // LANES):
                first = q * part + j * LANES
                d_weight[c * half : (c + 1) * half, first : first + LANES] = flat[
                    j * half : (j + 1) * half
                ].astype(BF)


def project_body(w_all, grads, d_attn, w_in, grads_in, sem_w, sem):
    load = pltpu.make_async_copy(grads, grads_in, sem.at[0])
    w_loads = [pltpu.make_async_copy(w_all.at[h], w_in.at[h], sem_w.at[h]) for h in range(HEADS)]
    load.start()
    for w_load in w_loads:
        w_load.start()
    load.wait()
    for w_load in w_loads:
        w_load.wait()
    for h in range(HEADS):
        d_attn[:, h * HD : (h + 1) * HD] = nt(grads_in[...], w_in[h]).astype(BF)


def attention_body(counts, adjacency, d_attn, behind, ahead, *refs):
    sources, rest = refs[:4], refs[4:]
    targets, rest = rest[:4], rest[4:]
    arrays, rest = rest[:4], rest[4:]
    results, (sem_in, sem_out) = rest[:4], rest[4:]
    queries, keys, attn_out, values = arrays
    d_queries, own, to_behind, to_ahead = results
    rows = queries.shape[0]
    loads = [
        pltpu.make_async_copy(source, array, sem_in.at[i])
        for i, (source, array) in enumerate(zip(sources, arrays))
    ]
    for load in loads:
        load.start()
    for load in loads:
        load.wait()
    allowed = allowed_pairs(counts, adjacency, behind, ahead, rows)
    for h in range(HEADS):
        cols = slice(h * HD, (h + 1) * HD)
        key_win = jnp.concatenate([behind[0:rows, cols], keys[:, cols], ahead[0:rows, cols]], 0)
        query = queries[:, cols]
        scores = jnp.where(allowed, nt(query, key_win) * SCALE, -1e30)
        terms = jnp.exp(scores - jnp.max(scores, axis=1, keepdims=True))
        terms = jnp.where(allowed, terms, 0.0)
        prob = terms / jnp.sum(terms, axis=1, keepdims=True)
        grad = d_attn[:, cols]
        delta = jnp.sum(
            grad.astype(F32) * attn_out[:, cols].astype(F32), axis=1, keepdims=True
        )
        value_win = jnp.concatenate(
            [behind[rows : 2 * rows, cols], values[:, cols], ahead[rows : 2 * rows, cols]], 0
        )
        dprobs = nt(grad, value_win)
        dscores = (prob * (dprobs - delta) * SCALE).astype(BF)
        d_queries[:, cols] = nn(dscores, key_win).astype(BF)
        for which, (left, right) in enumerate(((dscores, query), (prob.astype(BF), grad))):
            win = tn(left, right)
            to_behind[which, :, cols] = win[:rows].astype(BF)
            own[which, :, cols] = win[rows : 2 * rows]
            to_ahead[which, :, cols] = win[2 * rows :].astype(BF)
    stores = [
        pltpu.make_async_copy(result, target, sem_out.at[i])
        for i, (result, target) in enumerate(zip(results, targets))
    ]
    for store in stores:
        store.start()
    for store in stores:
        store.wait()


def finish_body(own, from_behind, from_ahead, d_keys, d_values):
    for which, out in enumerate((d_keys, d_values)):
        out[...] = (
            own[which] + from_behind[which].astype(F32) + from_ahead[which].astype(F32)
        ).astype(BF)


def vmem():
    return pl.BlockSpec(memory_space=pltpu.VMEM)


def smem():
    return pl.BlockSpec(memory_space=pltpu.SMEM)


def hbm():
    return pl.BlockSpec(memory_space=pltpu.HBM)


def in_hbm(value):
    return pltpu.with_memory_space_constraint(value, pltpu.HBM)


PARAMS = pltpu.CompilerParams(vmem_limit_bytes=20 << 20)


def call(body, outs, specs, scratch=()):
    return pl.pallas_call(
        body,
        out_shape=tuple(jax.ShapeDtypeStruct(shape, dtype) for shape, dtype in outs),
        in_specs=specs,
        out_specs=tuple(vmem() for _ in outs),
        scratch_shapes=scratch,
        compiler_params=PARAMS,
    )


def shift(value, by):
    length = lax.axis_size(REGION)
    return lax.ppermute(value, REGION, [(i, (i + by) % length) for i in range(length)])


def spread_out(value, ways):
    return jnp.broadcast_to(value[None], (ways,) + value.shape)


def local(queries, keys, values, attn_out, d_out, w_out, adjacency, counts):
    queries, keys, values, attn_out, d_out = (
        a[0] for a in (queries, keys, values, attn_out, d_out)
    )
    rows, hw = queries.shape
    width = d_out.shape[1]
    samples = lax.axis_size(DP)
    cores = lax.axis_size("core")
    chips = lax.axis_size("y")
    down = lax.axis_size("x")
    across = lax.axis_size("z_hi")
    part = width // down
    half = HD // cores

    core = lax.axis_index("core").reshape(1)
    w_half, spread, grads, halo = pl.pallas_call(
        prepare_body,
        out_shape=(
            pltpu.HBM((half, width), BF),
            pltpu.HBM((samples, 2 * rows, part), BF),
            pltpu.HBM((rows, width), BF),
            pltpu.HBM((2 * rows + 8, hw), BF),
        ),
        in_specs=[smem()] * 2 + [hbm()] * 5,
        out_specs=(hbm(),) * 4,
        scratch_shapes=[
            pltpu.VMEM((half, width), BF),
            pltpu.VMEM((rows, width), BF),
            pltpu.VMEM((rows, hw), BF),
            pltpu.VMEM((8, hw), BF),
            pltpu.VMEM((2 * rows, hw), BF),
            pltpu.SemaphoreType.DMA((5,)),
            pltpu.SemaphoreType.DMA((samples,)),
            pltpu.SemaphoreType.DMA((samples,)),
            pltpu.SemaphoreType.DMA((4,)),
        ],
        compiler_params=PARAMS,
    )(counts, core, *(in_hbm(a) for a in (d_out, attn_out, keys, values, w_out)))
    w_all = lax.all_gather(w_half, DP + ("core",), axis=0, tiled=True)

    gathered = lax.all_to_all(spread, DP, 0, 0)

    group = 2
    share = -(-(half * part // LANES) // (8 * chips)) * 8
    pieces = (cores, chips, down, share, LANES)
    weight = pl.pallas_call(
        weight_body,
        out_shape=jax.ShapeDtypeStruct(pieces, BF),
        grid=(samples // group,),
        in_specs=[pl.BlockSpec((group, 2 * rows, part), lambda i: (i, 0, 0))],
        out_specs=pl.BlockSpec(pieces, lambda i: (0, 0, 0, 0, 0)),
        scratch_shapes=[pltpu.VMEM((part, part), F32)],
        compiler_params=PARAMS,
    )(gathered)

    pair = lax.all_to_all(weight, "core", 0, 0)
    terms = jnp.sum(pair.astype(F32), axis=0).astype(BF)
    terms, halo, grads = lax.optimization_barrier((terms, halo, grads))
    (d_attn,) = call(
        project_body,
        [((rows, hw), BF)],
        [hbm(), hbm()],
        [
            pltpu.VMEM((HEADS, HD, width), BF),
            pltpu.VMEM((rows, width), BF),
            pltpu.SemaphoreType.DMA((HEADS,)),
            pltpu.SemaphoreType.DMA((1,)),
        ],
    )(in_hbm(w_all.reshape(HEADS, HD, width)), in_hbm(grads))
    behind = shift(halo, 1)
    ahead = shift(halo, -1)
    terms = lax.all_to_all(terms, "y", 0, 0)
    terms, d_attn = lax.optimization_barrier((terms, d_attn))
    terms = jnp.sum(terms.astype(F32), axis=0).astype(BF)
    terms = jnp.broadcast_to(terms[:, None], (down, across, share, LANES))
    terms = terms.reshape(down * across, share, LANES)
    terms, d_attn = lax.optimization_barrier((terms, d_attn))
    operands = (queries, keys, attn_out, values)
    pairs = (2, rows, hw)
    results = (((rows, hw), BF), (pairs, F32), (pairs, BF), (pairs, BF))
    d_queries, own, to_behind, to_ahead = pl.pallas_call(
        attention_body,
        out_shape=tuple(pltpu.HBM(shape, dtype) for shape, dtype in results),
        in_specs=[smem()] * 2 + [vmem()] * 3 + [hbm()] * len(operands),
        out_specs=(hbm(),) * len(results),
        scratch_shapes=[pltpu.VMEM(a.shape, a.dtype) for a in operands]
        + [pltpu.VMEM(shape, dtype) for shape, dtype in results]
        + [
            pltpu.SemaphoreType.DMA((len(operands),)),
            pltpu.SemaphoreType.DMA((len(results),)),
        ],
        compiler_params=PARAMS,
    )(counts, adjacency[0], d_attn, behind, ahead, *(in_hbm(a) for a in operands))
    terms = lax.all_to_all(terms, ("x", "z_hi"), 0, 0).reshape(down, across, share, LANES)
    terms, own = lax.optimization_barrier((terms, own))
    total = jnp.sum(terms.astype(F32), axis=1).astype(BF)
    total = lax.all_to_all(spread_out(total, chips), "y", 0, 0)
    both = lax.all_to_all(spread_out(total, cores), "core", 0, 0)
    (d_weight,) = call(assemble_body, [((HD, width), BF)], [vmem()])(both)

    d_weight, own = lax.optimization_barrier((d_weight, own))
    d_keys, d_values = call(
        finish_body, [((rows, hw), BF), ((rows, hw), BF)], [vmem()] * 3
    )(own, shift(to_ahead, 1), shift(to_behind, -1))
    return d_queries[None], d_keys[None], d_values[None], d_weight


def solution(mesh):
    parts = Mesh(mesh.devices.reshape(2, 4, 8, 4, 2), DP + REGION)
    rows = P(DP, REGION, None)
    return jax.shard_map(
        local,
        mesh=parts,
        in_specs=(rows, rows, rows, rows, rows, P(DP, None), P(REGION, None, None), P(REGION)),
        out_specs=(rows, rows, rows, P(DP, None)),
        check_vma=False,
    )
```
